32 devices in a mesh: ctx: 8 (over y, x, core), chan: 4 (over z).
Axes of the slice: x: 2, y: 2, z: 4, core: 2. Of those that a mesh axis runs over, the one named last changes fastest.
Arguments:
- value_branch: bfloat16 [192, 65536], P(None, ('ctx', 'chan')), may hold values from -6 to 6
- key_branch: bfloat16 [192, 65536], P(None, ('ctx', 'chan')), may hold values from -6 to 6
- gate_branch: bfloat16 [192, 65536], P(None, ('ctx', 'chan')), may hold values from -6 to 6
- skip_gain: float32 [192], replicated, may hold values from -4 to 4
- spectra: float32 [2, 192, 8, 8192], P(None, 'chan', 'ctx'), may hold values from -6 to 6
Outputs:
- gated_output: bfloat16 [192, 65536], P(None, ('ctx', 'chan'))
The draws below stay inside these ranges and needn't reach their ends.
All inputs are finite; a program needn't handle non-finite values.
Results may differ from the reference program's by a relative error of at most 0.0054.
Values may be sent and summed in bfloat16 or wider, within the bound.
A program may use at most 64 MiB of HBM per device.

```python
import jax
import jax.numpy as jnp
import numpy as np
from jax import lax

CHANNELS = 192
SEQ_DEV = 8192
LENGTH = 65536
N_CTX = 8


def steps_of(rng, shape, cuts, least, high):
    level, own = 1.0, jax.random.fold_in(rng, 6)
    for dim, blocks in cuts:
        steps = jnp.exp(jax.random.uniform(jax.random.fold_in(own, dim), (blocks,), jnp.float32, least / len(cuts), high / len(cuts)))
        level = level * jnp.repeat(steps, shape[dim] // blocks).reshape([-1 if axis == dim else 1 for axis in range(len(shape))])
    return level


def scatter_about(key, dims, width, most, cuts=(), held_as=jnp.bfloat16):
    entries = width * jax.random.normal(key, dims, jnp.float32)
    if cuts:
        entries = entries * steps_of(key, dims, cuts, -0.22, 0.18)
    return jnp.clip(entries, -most, most).astype(held_as)


def setup_inputs(seed: int = 0) -> dict:
    keys = jax.random.split(jax.random.key(seed), 6)
    value_branch = scatter_about(keys[0], (CHANNELS, LENGTH), 1.0, 6.0, ((1, 32),))
    key_branch = scatter_about(keys[1], (CHANNELS, LENGTH), 1.0, 6.0, ((1, 32),))
    gate_branch = scatter_about(keys[2], (CHANNELS, LENGTH), 1.0, 6.0, ((1, 32),))
    skip_gain = scatter_about(keys[3], (CHANNELS,), 1.0, 4.0, (), jnp.float32)
    spectra = scatter_about(keys[4], (2, CHANNELS, N_CTX, SEQ_DEV), 1.0, 6.0, ((1, 4), (2, 8)), jnp.float32)
    return dict(value_branch=value_branch, key_branch=key_branch, gate_branch=gate_branch, skip_gain=skip_gain, spectra=spectra)


def reversed_bits(numbers, bit_count):
    result = numbers * 0
    for bit_number in range(bit_count):
        result = result + ((numbers >> bit_number) & 1) * (1 << (bit_count - 1 - bit_number))
    return result


def reference(value_branch, key_branch, gate_branch, skip_gain, spectra):
    carried = (key_branch.astype(jnp.float32) * value_branch.astype(jnp.float32)).astype(jnp.bfloat16)
    bit_count = N_CTX.bit_length() - 1
    reversed_order = reversed_bits(np.arange(N_CTX), bit_count)

    def convolve(packed):
        signal, filter_real, filter_imag = packed
        natural_real = jnp.swapaxes(filter_real[reversed_order, :], 0, 1).reshape(-1)
        natural_imag = jnp.swapaxes(filter_imag[reversed_order, :], 0, 1).reshape(-1)
        transformed = jnp.fft.fft(signal.astype(jnp.float32))
        shaped = transformed * (natural_real + 1j * natural_imag)
        return jnp.real(jnp.fft.ifft(shaped)).astype(jnp.float32)

    convolved = lax.map(convolve, (carried, spectra[0], spectra[1])).astype(jnp.bfloat16)
    result = gate_branch.astype(jnp.float32) * (convolved.astype(jnp.float32) + skip_gain[:, None] * carried.astype(jnp.float32))
    return result.astype(jnp.bfloat16)
```

```python
import functools
import math

import jax
import jax.numpy as jnp
import numpy as np
from jax import lax
from jax.experimental import pallas as pl
from jax.experimental.pallas import tpu as pltpu
from jax.sharding import PartitionSpec as P

two_pi = 2.0 * math.pi
first_factor = 128
highest = lax.Precision.HIGHEST


def reversed_bits(numbers, bit_count):
    result = numbers * 0
    for bit_number in range(bit_count):
        result = result + (numbers >> bit_number & 1) * (1 << bit_count - 1 - bit_number)
    return result


def phase_pair(radians):
    return (jnp.cos(radians), jnp.sin(radians))


def block_table(length_of, direction):
    counter = jnp.arange(length_of, dtype=jnp.int32)
    product = counter[:, None] * counter[None, :] % length_of
    cosine, sine = phase_pair(direction * two_pi / length_of * product.astype(jnp.float32))
    upper_rows = jnp.stack([cosine, -sine], axis=1)
    lower_rows = jnp.stack([sine, cosine], axis=1)
    return jnp.stack([upper_rows, lower_rows], axis=0)


def complex_mul(signal, factor):
    factor_real, factor_imag = factor
    return jnp.stack(
        [
            signal[0] * factor_real - signal[1] * factor_imag,
            signal[0] * factor_imag + signal[1] * factor_real,
        ]
    )


def forward_local(signal):
    channel_count, seq_length = (signal.shape[1], signal.shape[2])
    second_factor = seq_length // first_factor
    blocked = signal.reshape(2, channel_count, first_factor, second_factor)
    section_one = jnp.einsum(
        "orca,cxaq->oxrq", block_table(first_factor, -1.0), blocked, precision=highest
    )
    column = jnp.arange(first_factor, dtype=jnp.int32)[:, None]
    within = jnp.arange(second_factor, dtype=jnp.int32)[None, :]
    twiddle = phase_pair(-two_pi / seq_length * (column * within).astype(jnp.float32))
    section_two = complex_mul(section_one, twiddle)
    section_three = jnp.einsum(
        "peoq,oxrq->pxer", block_table(second_factor, -1.0), section_two, precision=highest
    )
    return section_three.reshape(2, channel_count, seq_length)


def inverse_local(signal):
    channel_count, seq_length = (signal.shape[1], signal.shape[2])
    second_factor = seq_length // first_factor
    blocked = signal.reshape(2, channel_count, second_factor, first_factor)
    section_one = jnp.einsum(
        "pqoe,oxer->pxqr", block_table(second_factor, 1.0), blocked, precision=highest
    )
    within = jnp.arange(second_factor, dtype=jnp.int32)[:, None]
    column = jnp.arange(first_factor, dtype=jnp.int32)[None, :]
    twiddle = phase_pair(two_pi / seq_length * (within * column).astype(jnp.float32))
    section_two = complex_mul(section_one, twiddle)
    section_three = jnp.einsum(
        "paor,oxqr->pxaq", block_table(first_factor, 1.0), section_two, precision=highest
    )
    return section_three.reshape(2, channel_count, seq_length)


def blockwise_body(value_branch, key_branch, gate_branch, skip_gain, spectra):
    carried = (key_branch.astype(jnp.float32) * value_branch.astype(jnp.float32)).astype(
        jnp.bfloat16
    )
    series = lax.all_to_all(carried, "chan", split_axis=0, concat_axis=1, tiled=True)
    channel_count, seq_length = series.shape
    ctx_count = lax.axis_size("ctx")
    bit_count = ctx_count.bit_length() - 1
    device = lax.axis_index("ctx")
    total_length = seq_length * ctx_count
    counter = jnp.arange(ctx_count, dtype=jnp.int32)
    target = reversed_bits(counter, bit_count)
    blocks = lax.all_to_all(
        series.reshape(channel_count, 1, seq_length), "ctx", split_axis=2, concat_axis=1, tiled=True
    )
    matrix = jnp.stack(
        phase_pair(
            -two_pi
            / ctx_count
            * (target[:, None] * counter[None, :] % ctx_count).astype(jnp.float32)
        )
    )
    rows = jnp.einsum("ojp,xps->oxjs", matrix, blocks.astype(jnp.float32), precision=highest)
    received = lax.all_to_all(rows, "ctx", split_axis=2, concat_axis=3, tiled=True)
    signal = received.reshape(2, channel_count, seq_length)
    device_rank = reversed_bits(device, bit_count)
    positions = jnp.arange(seq_length, dtype=jnp.int32)
    radians = two_pi / total_length * (positions * device_rank).astype(jnp.float32)
    signal = complex_mul(signal, phase_pair(-radians))
    spectrum = forward_local(signal)
    shaped = complex_mul(spectrum, (spectra[0, :, 0, :], spectra[1, :, 0, :]))
    returned = complex_mul(inverse_local(shaped), phase_pair(radians))
    parts = lax.all_to_all(
        returned.reshape(2, channel_count, 1, seq_length),
        "ctx",
        split_axis=3,
        concat_axis=2,
        tiled=True,
    )
    cosine, sine = phase_pair(
        two_pi / ctx_count * (counter[:, None] * target[None, :] % ctx_count).astype(jnp.float32)
    )
    matrix = jnp.stack([cosine, -sine])
    summed = jnp.einsum("opj,oxjs->xps", matrix, parts, precision=highest) / total_length
    local_conv = summed.astype(jnp.bfloat16)
    convolved = lax.all_to_all(local_conv, "ctx", split_axis=1, concat_axis=2, tiled=True).reshape(
        channel_count, seq_length
    )
    tokens_conv = lax.all_to_all(convolved, "chan", split_axis=1, concat_axis=0, tiled=True)
    result = gate_branch.astype(jnp.float32) * (
        tokens_conv.astype(jnp.float32) + skip_gain[:, None] * carried.astype(jnp.float32)
    )
    return result.astype(jnp.bfloat16)


lanes = 128
MESH = pl.DeviceIdType.MESH
VMEM = pl.BlockSpec(memory_space=pltpu.VMEM)


@functools.lru_cache(maxsize=None)
def transform_tables(rows_total, ctx_count, least_bytes):
    length = rows_total * lanes
    bit_count = ctx_count.bit_length() - 1
    rev = np.array([int(format(j, "b").zfill(bit_count)[::-1], 2) if bit_count else 0 for j in range(ctx_count)])
    a = np.arange(rows_total // ctx_count)
    k1 = (rev[:, None] + ctx_count * a[None, :]).reshape(-1)
    fold = lanes // (rows_total // ctx_count)
    k2 = np.arange(lanes).reshape(lanes // fold, fold).T.reshape(-1)
    n1, n2 = np.arange(rows_total), np.arange(lanes)
    f1 = np.exp(-2j * np.pi * (np.outer(k1, n1) % rows_total) / rows_total)
    f2 = np.exp(-2j * np.pi * (np.outer(n2, k2) % lanes) / lanes)
    tw = np.exp(-2j * np.pi * (np.outer(k1, n2) % length) / length)
    w1 = np.stack([f1.real, f1.imag])
    w2 = np.block([[f2.real, f2.imag], [-f2.imag, f2.real]])
    b2 = f2.conj().T
    w3 = np.block([[b2.real, b2.imag], [-b2.imag, b2.real]])
    b1 = f1.conj().T / length
    v1 = np.concatenate([b1.real, -b1.imag], axis=1)
    half = lambda t: np.asarray(t, dtype=jnp.bfloat16)
    pieces = [w1.reshape(2 * rows_total, rows_total), v1[:, :rows_total], v1[:, rows_total:]]
    square = np.concatenate([w2, w3], axis=1)
    pieces.append(np.pad(square, ((0, 0), (0, max(rows_total - square.shape[1], 0)))))
    turns = np.stack([tw.real, tw.imag]).astype(np.float32)
    spare = np.zeros((2 * (least_bytes // turns.nbytes),) + turns.shape[1:], np.float32)
    return np.concatenate(pieces).astype(jnp.bfloat16), np.concatenate([turns, spare])


def greet_all(ctx_count, chan_count, me):
    total = ctx_count * chan_count
    barrier = pltpu.get_barrier_semaphore()

    @pl.loop(1, total)
    def _(offset):
        other = lax.rem(me + offset, total)
        pl.semaphore_signal(
            barrier, inc=1, device_id=(other // chan_count, lax.rem(other, chan_count)), device_id_type=MESH
        )


def dot(a, b):
    return jnp.dot(a, b, preferred_element_type=jnp.float32)


def fused_kernel(ctx_count, chan_count, skip_hbm, v_hbm, k_hbm, gate_hbm, s_hbm, table_hbm, tw_hbm, out_ref, *refs):
    skip_ref, w1_ref, w2_ref, w3_ref, v1_ref, tw_ref = refs[:6]
    s_ref, stage, r_ref, x_ref, y_ref, g_ref, b_ref = refs[6:13]
    v_ref, k_ref, gate_ref, c_ref, o_ref = refs[13:18]
    sent, got_c, got_s, got_y, local = refs[18:]
    ctx, chan = lax.axis_index("ctx"), lax.axis_index("chan")
    me = ctx * chan_count + chan
    total = ctx_count * chan_count
    pairs, rows = x_ref.shape[0], c_ref.shape[1]
    rows_total = x_ref.shape[1]
    block = stage.shape[2]
    local_channels = stage.shape[1]
    wide = 2 * lanes

    def load(index, source, target):
        return pltpu.make_async_copy(source, target, local.at[index])

    first_rows = 2 * rows_total
    loads = [
        load(0, v_hbm, v_ref),
        load(1, k_hbm, k_ref),
        load(2, s_hbm, s_ref),
        load(3, table_hbm.at[pl.ds(0, first_rows)], w1_ref),
        load(4, table_hbm.at[pl.ds(2 * first_rows, wide), pl.ds(0, wide)], w2_ref),
        load(5, table_hbm.at[pl.ds(2 * first_rows, wide), pl.ds(wide, wide)], w3_ref),
        load(6, tw_hbm.at[pl.ds(0, 2)], tw_ref),
        load(7, table_hbm.at[pl.ds(first_rows, rows_total)], v1_ref.at[:, pl.ds(0, rows_total)]),
        load(8, table_hbm.at[pl.ds(first_rows + rows_total, rows_total)], v1_ref.at[:, pl.ds(rows_total, rows_total)]),
        load(9, gate_hbm, gate_ref),
        load(10, skip_hbm, skip_ref),
    ]
    loads[0].start()
    loads[1].start()
    greet_all(ctx_count, chan_count, me)
    for copy in loads[2:]:
        copy.start()
    group = 2 * ctx_count

    def pack(pair):
        @pl.loop(0, chan_count)
        def _(chan_index):
            index = chan_index * pairs + pair
            at = pl.ds(pl.multiple_of(index * group, group), group)
            product = (k_ref[at].astype(jnp.float32) * v_ref[at].astype(jnp.float32)).astype(jnp.bfloat16)
            split = product.astype(jnp.float32).reshape(ctx_count, 2, rows, lanes)
            packed = jnp.concatenate([split[:, 0], split[:, 1]], axis=2)
            c_ref[pl.ds(index * ctx_count, ctx_count)] = packed.astype(jnp.bfloat16)

    def place(offset):
        other = lax.rem(me + offset, total)
        return other, other // chan_count, lax.rem(other, chan_count)

    def slot(ctx_index, chan_index, pair):
        return (chan_index * pairs + pair) * ctx_count + ctx_index

    my_rows = pl.ds(pl.multiple_of(me * rows, rows), rows)
    my_block = pl.ds(pl.multiple_of(ctx * block, block), block)

    def carried_copy(pair, offset):
        other, other_ctx, other_chan = place(offset)
        return pltpu.make_async_remote_copy(
            src_ref=c_ref.at[slot(other_ctx, other_chan, pair)],
            dst_ref=x_ref.at[pair, my_rows],
            send_sem=sent.at[0],
            recv_sem=got_c.at[pair],
            device_id=(other_ctx, other_chan),
            device_id_type=MESH,
        )

    def spectra_copy(pair, first, count, offset):
        other_ctx = lax.rem(ctx + offset, ctx_count)
        return pltpu.make_async_remote_copy(
            src_ref=stage.at[:, pl.ds((pair * ctx_count + other_ctx) * 2 + first, count)],
            dst_ref=r_ref.at[:, pl.ds(2 * pair + first, count), my_block],
            send_sem=sent.at[1],
            recv_sem=got_s.at[2 * pair + first],
            device_id=(other_ctx, chan),
            device_id_type=MESH,
        )

    def columns(first, count):
        return pl.ds(first * lanes, count * lanes)

    def result_copy(pair, first, count, other):
        other_ctx, other_chan = other // chan_count, lax.rem(other, chan_count)
        return pltpu.make_async_remote_copy(
            src_ref=y_ref.at[pair, pl.ds(pl.multiple_of(other * rows, rows), rows), columns(first, count)],
            dst_ref=o_ref.at[slot(ctx, chan, pair), :, columns(first, count)],
            send_sem=sent.at[2],
            recv_sem=got_y.at[pair],
            device_id=(other_ctx, other_chan),
            device_id_type=MESH,
        )

    def settle(ref, sem):
        pltpu.make_async_copy(ref, ref, sem).wait()

    def turned(part, channel):
        flipped = s_ref[part * local_channels + channel].T
        pieces = [flipped[f * block : (f + 1) * block] for f in range(flipped.shape[0] // block)]
        return jnp.concatenate(pieces, axis=1).astype(jnp.bfloat16)

    def turn(pair):
        @pl.loop(1, ctx_count)
        def _(offset):
            first = (pair * ctx_count + lax.rem(ctx + offset, ctx_count)) * 2
            for part in range(2):
                for which in range(2):
                    stage[part, first + which] = turned(part, first + which)

    def turn_own(pair):
        for part in range(2):
            for which in range(2):
                r_ref[part, 2 * pair + which, my_block] = turned(part, (pair * ctx_count + ctx) * 2 + which)
        x_ref[pair, my_rows] = c_ref[slot(ctx, chan, pair)]

    def send_carried(pair):
        @pl.loop(1, total)
        def _(offset):
            carried_copy(pair, offset).start()

    def send_spectra(pair, first, count):
        @pl.loop(1, ctx_count)
        def _(offset):
            spectra_copy(pair, first, count, offset).start()

    chunk = 2 * lanes

    def forward(pair):
        settle(c_ref.at[pl.ds(0, total - 1)], got_c.at[pair])
        x = x_ref.at[pair]

        @pl.loop(0, rows_total // chunk)
        def _(step):
            at = pl.ds(pl.multiple_of(step * chunk, chunk), chunk)
            below = pl.ds(pl.multiple_of(rows_total + step * chunk, chunk), chunk)
            real, imag = dot(w1_ref[at], x[...]), dot(w1_ref[below], x[...])
            t_real, t_imag = tw_ref[0, at], tw_ref[1, at]
            for which in range(2):
                cols = slice(which * lanes, (which + 1) * lanes)
                a_real, a_imag = real[:, cols], imag[:, cols]
                twiddled = jnp.concatenate(
                    [a_real * t_real - a_imag * t_imag, a_real * t_imag + a_imag * t_real], axis=1
                )
                b_ref[2 * pair + which, at] = dot(twiddled.astype(jnp.bfloat16), w2_ref[...])

    def backward(pair, first, count):
        settle(stage.at[:, pl.ds(0, count * (ctx_count - 1))], got_s.at[2 * pair + first])

        @pl.loop(0, rows_total // chunk)
        def _(step):
            at = pl.ds(pl.multiple_of(step * chunk, chunk), chunk)
            below = pl.ds(pl.multiple_of(rows_total + step * chunk, chunk), chunk)
            t_real, t_imag = tw_ref[0, at], tw_ref[1, at]
            for which in range(first, first + count):
                cols = slice(which * lanes, (which + 1) * lanes)
                bins = b_ref[2 * pair + which, at]
                b_real, b_imag = bins[:, :lanes], bins[:, lanes:]
                f_real = r_ref[0, 2 * pair + which, at].astype(jnp.float32)
                f_imag = r_ref[1, 2 * pair + which, at].astype(jnp.float32)
                shaped = jnp.concatenate(
                    [b_real * f_real - b_imag * f_imag, b_real * f_imag + b_imag * f_real], axis=1
                )
                back = dot(shaped.astype(jnp.bfloat16), w3_ref[...])
                z_real, z_imag = back[:, :lanes], back[:, lanes:]
                g_ref[at, cols] = (z_real * t_real + z_imag * t_imag).astype(jnp.bfloat16)
                g_ref[below, cols] = (z_imag * t_real - z_real * t_imag).astype(jnp.bfloat16)

        steps = rows_total // chunk
        spread = total // steps
        home = me // spread
        cols = slice(first * lanes, (first + count) * lanes)

        @pl.loop(0, steps)
        def _(step):
            turn_of = lax.rem(home + 1 + step, steps)
            at = pl.ds(pl.multiple_of(turn_of * chunk, chunk), chunk)
            y_ref[pair, at, cols] = dot(v1_ref[at], g_ref[:, cols]).astype(jnp.bfloat16)

            @pl.loop(0, spread)
            def _(index):
                other = turn_of * spread + lax.rem(me + 1 + index, spread)

                @pl.when(other != me)
                def _():
                    result_copy(pair, first, count, other).start()

        o_ref[slot(ctx, chan, pair), :, cols] = y_ref[pair, my_rows, cols]

    def finish(pair):
        settle(o_ref.at[pl.ds(0, total - 1)], got_y.at[pair])

        @pl.loop(0, chan_count)
        def _(chan_index):
            first = slot(0, chan_index, pair)
            sums = []
            for i in range(ctx_count):
                for which in range(2):
                    cols = slice(which * lanes, (which + 1) * lanes)
                    carried = c_ref[first + i, :, cols].astype(jnp.float32)
                    gain = skip_ref[2 * (first + i) + which]
                    sums.append(o_ref[first + i, :, cols].astype(jnp.float32) + gain * carried)
            flat = jnp.stack(sums).reshape(group, rows * lanes)
            at = pl.ds(pl.multiple_of(first * 2, group), group)
            out_ref[at] = (gate_ref[at].astype(jnp.float32) * flat).astype(jnp.bfloat16)

    waited = set()

    def need(*indices):
        for index in indices:
            if index not in waited:
                waited.add(index)
                loads[index].wait()

    need(0, 1)
    pack(0)
    need(0, 1)
    pack(1)
    need(0, 1)
    pack(2)
    pl.semaphore_wait(pltpu.get_barrier_semaphore(), total - 1)
    send_carried(0)
    send_carried(1)
    send_carried(2)
    need(2)
    turn(0)
    send_spectra(0, 0, 2)
    need(2)
    turn_own(0)
    need(2)
    turn(1)
    send_spectra(1, 0, 2)
    need(2)
    turn_own(1)
    need(2)
    turn(2)
    send_spectra(2, 0, 1)
    send_spectra(2, 1, 1)
    need(2)
    turn_own(2)
    need(3, 4, 6)
    forward(0)
    need(3, 4, 6)
    forward(1)
    need(5, 7, 8)
    backward(0, 0, 2)
    need(3, 4, 6)
    forward(2)
    need(5, 7, 8)
    backward(1, 0, 2)
    need(5, 7, 8)
    backward(2, 0, 1)
    need(5, 7, 8)
    backward(2, 1, 1)
    need(9, 10)
    finish(0)
    need(9, 10)
    finish(1)
    need(9, 10)
    finish(2)
    settle(c_ref.at[pl.ds(0, pairs * (total - 1))], sent.at[0])
    settle(stage.at[:, pl.ds(0, 2 * pairs * (ctx_count - 1))], sent.at[1])
    settle(o_ref.at[pl.ds(0, pairs * (total - 1))], sent.at[2])


def channel_body(value_branch, key_branch, gate_branch, skip_gain, spectra):
    channels, tokens = value_branch.shape
    ctx_count, chan_count = lax.axis_size("ctx"), lax.axis_size("chan")
    total = ctx_count * chan_count
    rows = tokens // lanes
    rows_total = rows * total
    pairs = channels // total // 2
    local_channels = spectra.shape[1]
    block = spectra.shape[3] // lanes
    table, turns = [jnp.asarray(t) for t in transform_tables(rows_total, ctx_count, 2 * channels * tokens)]
    sems = lambda *shape: pltpu.SemaphoreType.DMA(shape)
    hbm = pl.BlockSpec(memory_space=pl.ANY)
    packed = pltpu.VMEM((channels // 2, rows, 2 * lanes), jnp.bfloat16)
    held = pltpu.VMEM((channels, tokens), jnp.bfloat16)
    half = lambda *shape: pltpu.VMEM(shape, jnp.bfloat16)
    return pl.pallas_call(
        functools.partial(fused_kernel, ctx_count, chan_count),
        in_specs=[hbm] * 7,
        out_specs=VMEM,
        out_shape=jax.ShapeDtypeStruct((channels, tokens), jnp.bfloat16),
        scratch_shapes=[
            pltpu.SMEM((channels,), jnp.float32),
            half(2 * rows_total, rows_total),
            half(2 * lanes, 2 * lanes),
            half(2 * lanes, 2 * lanes),
            half(rows_total, 2 * rows_total),
            pltpu.VMEM((2, rows_total, lanes), jnp.float32),
            pltpu.VMEM((2 * local_channels, block, lanes), jnp.float32),
            half(2, local_channels, block, lanes),
            half(2, 2 * pairs, rows_total, lanes),
            half(pairs, rows_total, 2 * lanes),
            half(pairs, rows_total, 2 * lanes),
            half(2 * rows_total, 2 * lanes),
            pltpu.VMEM((2 * pairs, rows_total, 2 * lanes), jnp.float32),
            held, held, held, packed, packed,
            sems(3), sems(pairs), sems(2 * pairs), sems(pairs), sems(11),
        ],
        compiler_params=pltpu.CompilerParams(collective_id=0, has_side_effects=True, vmem_limit_bytes=55369728),
    )(
        skip_gain,
        value_branch,
        key_branch,
        gate_branch,
        spectra.reshape(2 * local_channels, block, lanes),
        table,
        turns,
    )


def body(value_branch, key_branch, gate_branch, skip_gain, spectra):
    channels, tokens = value_branch.shape
    ctx_count, chan_count = lax.axis_size("ctx"), lax.axis_size("chan")
    total = ctx_count * chan_count
    block_rows = tokens * chan_count // lanes
    fits = (
        channels % (2 * total) == 0
        and ctx_count % 8 == 0
        and tokens % (16 * lanes) == 0
        and block_rows <= lanes
        and lanes % block_rows == 0
        and (tokens * total // lanes) % lanes == 0
    )
    chosen = channel_body if fits else blockwise_body
    return chosen(value_branch, key_branch, gate_branch, skip_gain, spectra)


def solution(mesh):
    in_specs = (
        P(None, ("ctx", "chan")),
        P(None, ("ctx", "chan")),
        P(None, ("ctx", "chan")),
        P(),
        P(None, "chan", "ctx", None),
    )
    out_specs = P(None, ("ctx", "chan"))
    return jax.shard_map(body, mesh=mesh, in_specs=in_specs, out_specs=out_specs, check_vma=False)
```

```python
import functools
import math

import jax
import jax.numpy as jnp
import numpy as np
from jax import lax
from jax.experimental import pallas as pl
from jax.experimental.pallas import tpu as pltpu
from jax.sharding import PartitionSpec as P

two_pi = 2.0 * math.pi
first_factor = 128
highest = lax.Precision.HIGHEST


def reversed_bits(numbers, bit_count):
    result = numbers * 0
    for bit_number in range(bit_count):
        result = result + (numbers >> bit_number & 1) * (1 << bit_count - 1 - bit_number)
    return result


def phase_pair(radians):
    return (jnp.cos(radians), jnp.sin(radians))


def block_table(length_of, direction):
    counter = jnp.arange(length_of, dtype=jnp.int32)
    product = counter[:, None] * counter[None, :] % length_of
    cosine, sine = phase_pair(direction * two_pi / length_of * product.astype(jnp.float32))
    upper_rows = jnp.stack([cosine, -sine], axis=1)
    lower_rows = jnp.stack([sine, cosine], axis=1)
    return jnp.stack([upper_rows, lower_rows], axis=0)


def complex_mul(signal, factor):
    factor_real, factor_imag = factor
    return jnp.stack(
        [
            signal[0] * factor_real - signal[1] * factor_imag,
            signal[0] * factor_imag + signal[1] * factor_real,
        ]
    )


def forward_local(signal):
    channel_count, seq_length = (signal.shape[1], signal.shape[2])
    second_factor = seq_length // first_factor
    blocked = signal.reshape(2, channel_count, first_factor, second_factor)
    section_one = jnp.einsum(
        "orca,cxaq->oxrq", block_table(first_factor, -1.0), blocked, precision=highest
    )
    column = jnp.arange(first_factor, dtype=jnp.int32)[:, None]
    within = jnp.arange(second_factor, dtype=jnp.int32)[None, :]
    twiddle = phase_pair(-two_pi / seq_length * (column * within).astype(jnp.float32))
    section_two = complex_mul(section_one, twiddle)
    section_three = jnp.einsum(
        "peoq,oxrq->pxer", block_table(second_factor, -1.0), section_two, precision=highest
    )
    return section_three.reshape(2, channel_count, seq_length)


def inverse_local(signal):
    channel_count, seq_length = (signal.shape[1], signal.shape[2])
    second_factor = seq_length // first_factor
    blocked = signal.reshape(2, channel_count, second_factor, first_factor)
    section_one = jnp.einsum(
        "pqoe,oxer->pxqr", block_table(second_factor, 1.0), blocked, precision=highest
    )
    within = jnp.arange(second_factor, dtype=jnp.int32)[:, None]
    column = jnp.arange(first_factor, dtype=jnp.int32)[None, :]
    twiddle = phase_pair(two_pi / seq_length * (within * column).astype(jnp.float32))
    section_two = complex_mul(section_one, twiddle)
    section_three = jnp.einsum(
        "paor,oxqr->pxaq", block_table(first_factor, 1.0), section_two, precision=highest
    )
    return section_three.reshape(2, channel_count, seq_length)


def blockwise_body(value_branch, key_branch, gate_branch, skip_gain, spectra):
    carried = (key_branch.astype(jnp.float32) * value_branch.astype(jnp.float32)).astype(
        jnp.bfloat16
    )
    series = lax.all_to_all(carried, "chan", split_axis=0, concat_axis=1, tiled=True)
    channel_count, seq_length = series.shape
    ctx_count = lax.axis_size("ctx")
    bit_count = ctx_count.bit_length() - 1
    device = lax.axis_index("ctx")
    total_length = seq_length * ctx_count
    counter = jnp.arange(ctx_count, dtype=jnp.int32)
    target = reversed_bits(counter, bit_count)
    blocks = lax.all_to_all(
        series.reshape(channel_count, 1, seq_length), "ctx", split_axis=2, concat_axis=1, tiled=True
    )
    matrix = jnp.stack(
        phase_pair(
            -two_pi
            / ctx_count
            * (target[:, None] * counter[None, :] % ctx_count).astype(jnp.float32)
        )
    )
    rows = jnp.einsum("ojp,xps->oxjs", matrix, blocks.astype(jnp.float32), precision=highest)
    received = lax.all_to_all(rows, "ctx", split_axis=2, concat_axis=3, tiled=True)
    signal = received.reshape(2, channel_count, seq_length)
    device_rank = reversed_bits(device, bit_count)
    positions = jnp.arange(seq_length, dtype=jnp.int32)
    radians = two_pi / total_length * (positions * device_rank).astype(jnp.float32)
    signal = complex_mul(signal, phase_pair(-radians))
    spectrum = forward_local(signal)
    shaped = complex_mul(spectrum, (spectra[0, :, 0, :], spectra[1, :, 0, :]))
    returned = complex_mul(inverse_local(shaped), phase_pair(radians))
    parts = lax.all_to_all(
        returned.reshape(2, channel_count, 1, seq_length),
        "ctx",
        split_axis=3,
        concat_axis=2,
        tiled=True,
    )
    cosine, sine = phase_pair(
        two_pi / ctx_count * (counter[:, None] * target[None, :] % ctx_count).astype(jnp.float32)
    )
    matrix = jnp.stack([cosine, -sine])
    summed = jnp.einsum("opj,oxjs->xps", matrix, parts, precision=highest) / total_length
    local_conv = summed.astype(jnp.bfloat16)
    convolved = lax.all_to_all(local_conv, "ctx", split_axis=1, concat_axis=2, tiled=True).reshape(
        channel_count, seq_length
    )
    tokens_conv = lax.all_to_all(convolved, "chan", split_axis=1, concat_axis=0, tiled=True)
    result = gate_branch.astype(jnp.float32) * (
        tokens_conv.astype(jnp.float32) + skip_gain[:, None] * carried.astype(jnp.float32)
    )
    return result.astype(jnp.bfloat16)


lanes = 128
MESH = pl.DeviceIdType.MESH
VMEM = pl.BlockSpec(memory_space=pltpu.VMEM)


@functools.lru_cache(maxsize=None)
def transform_tables(rows_total, ctx_count, least_bytes):
    length = rows_total * lanes
    bit_count = ctx_count.bit_length() - 1
    rev = np.array([int(format(j, "b").zfill(bit_count)[::-1], 2) if bit_count else 0 for j in range(ctx_count)])
    a = np.arange(rows_total // ctx_count)
    k1 = (rev[:, None] + ctx_count * a[None, :]).reshape(-1)
    fold = lanes // (rows_total // ctx_count)
    k2 = np.arange(lanes).reshape(lanes // fold, fold).T.reshape(-1)
    n1, n2 = np.arange(rows_total), np.arange(lanes)
    f1 = np.exp(-2j * np.pi * (np.outer(k1, n1) % rows_total) / rows_total)
    f2 = np.exp(-2j * np.pi * (np.outer(n2, k2) % lanes) / lanes)
    tw = np.exp(-2j * np.pi * (np.outer(k1, n2) % length) / length)
    w1 = np.stack([f1.real, f1.imag])
    w2 = np.block([[f2.real, f2.imag], [-f2.imag, f2.real]])
    b2 = f2.conj().T
    w3 = np.block([[b2.real, b2.imag], [-b2.imag, b2.real]])
    b1 = f1.conj().T / length
    v1 = np.concatenate([b1.real, -b1.imag], axis=1)
    half = lambda t: np.asarray(t, dtype=jnp.bfloat16)
    pieces = [w1.reshape(2 * rows_total, rows_total), v1[:, :rows_total], v1[:, rows_total:]]
    square = np.concatenate([w2, w3], axis=1)
    pieces.append(np.pad(square, ((0, 0), (0, max(rows_total - square.shape[1], 0)))))
    turns = np.stack([tw.real, tw.imag]).astype(np.float32)
    spare = np.zeros((2 * (least_bytes // turns.nbytes),) + turns.shape[1:], np.float32)
    return np.concatenate(pieces).astype(jnp.bfloat16), np.concatenate([turns, spare])


def dot(a, b):
    return jnp.dot(a, b, preferred_element_type=jnp.float32)


def fused_kernel(ctx_count, chan_count, skip_hbm, v_hbm, k_hbm, gate_hbm, s_hbm, table_hbm, tw_hbm, out_ref, *refs):
    skip_ref, w1_ref, w2_ref, w3_ref, v1_ref, tw_ref = refs[:6]
    s_ref, stage, r_ref, x_ref, y_ref, g_ref, b_ref = refs[6:13]
    v_ref, k_ref, gate_ref, c_ref, o_ref = refs[13:18]
    sent, got_c, got_s, got_y, local, ready = refs[18:]
    ctx, chan = lax.axis_index("ctx"), lax.axis_index("chan")
    me = ctx * chan_count + chan
    total = ctx_count * chan_count
    pairs, rows = x_ref.shape[0], c_ref.shape[1]
    rows_total = x_ref.shape[1]
    block = stage.shape[2]
    local_channels = stage.shape[1]
    wide = 2 * lanes

    def load(index, source, target):
        return pltpu.make_async_copy(source, target, local.at[index])

    first_rows = 2 * rows_total
    share = 2 * ctx_count
    rest = local_channels - share
    loads = [
        load(0, v_hbm, v_ref),
        load(1, k_hbm, k_ref),
        load(2, s_hbm.at[pl.ds(0, share)], s_ref.at[pl.ds(0, share)]),
        load(3, table_hbm.at[pl.ds(0, first_rows)], w1_ref),
        load(4, table_hbm.at[pl.ds(2 * first_rows, wide), pl.ds(0, wide)], w2_ref),
        load(5, table_hbm.at[pl.ds(2 * first_rows, wide), pl.ds(wide, wide)], w3_ref),
        load(6, tw_hbm.at[pl.ds(0, 2)], tw_ref),
        load(7, table_hbm.at[pl.ds(first_rows, rows_total)], v1_ref.at[:, pl.ds(0, rows_total)]),
        load(8, table_hbm.at[pl.ds(first_rows + rows_total, rows_total)], v1_ref.at[:, pl.ds(rows_total, rows_total)]),
        load(9, gate_hbm, gate_ref),
        load(10, skip_hbm, skip_ref),
        load(11, s_hbm.at[pl.ds(local_channels, share)], s_ref.at[pl.ds(local_channels, share)]),
        load(12, s_hbm.at[pl.ds(share, rest)], s_ref.at[pl.ds(share, rest)]),
        load(13, s_hbm.at[pl.ds(local_channels + share, rest)], s_ref.at[pl.ds(local_channels + share, rest)]),
    ]
    barrier = pltpu.get_barrier_semaphore()
    even = lax.rem(ctx, 2) == 0
    partner = (ctx + 1 - 2 * lax.rem(ctx, 2), chan)

    def signal(semaphore, device):
        pl.semaphore_signal(semaphore, inc=1, device_id=device, device_id_type=MESH)

    for index in (0, 1, 2, 11):
        loads[index].start()

    @pl.loop(0, ctx_count // 2)
    def _(chip):
        @pl.when(2 * chip != ctx)
        def _():
            signal(barrier, (2 * chip, chan))

        @pl.loop(1, chan_count)
        def _(offset):
            signal(barrier, (2 * chip + 1, lax.rem(chan + offset, chan_count)))

    for index in (12, 13, 3, 4, 6, 5, 7, 8, 9, 10):
        loads[index].start()
    group = 2 * ctx_count

    def pack(pair):
        @pl.loop(0, chan_count)
        def _(chan_index):
            index = chan_index * pairs + pair
            at = pl.ds(pl.multiple_of(index * group, group), group)
            product = (k_ref[at].astype(jnp.float32) * v_ref[at].astype(jnp.float32)).astype(jnp.bfloat16)
            split = product.astype(jnp.float32).reshape(ctx_count, 2, rows, lanes)
            packed = jnp.concatenate([split[:, 0], split[:, 1]], axis=2)
            c_ref[pl.ds(index * ctx_count, ctx_count)] = packed.astype(jnp.bfloat16)

    def place(offset):
        other = lax.rem(me + offset, total)
        return other, other // chan_count, lax.rem(other, chan_count)

    def slot(ctx_index, chan_index, pair):
        return (chan_index * pairs + pair) * ctx_count + ctx_index

    my_rows = pl.ds(pl.multiple_of(me * rows, rows), rows)
    my_block = pl.ds(pl.multiple_of(ctx * block, block), block)

    def carried_copy(pair, offset):
        other, other_ctx, other_chan = place(offset)
        return pltpu.make_async_remote_copy(
            src_ref=c_ref.at[slot(other_ctx, other_chan, pair)],
            dst_ref=x_ref.at[pair, my_rows],
            send_sem=sent.at[0],
            recv_sem=got_c.at[pair],
            device_id=(other_ctx, other_chan),
            device_id_type=MESH,
        )

    def spectra_copy(pair, first, count, offset):
        other_ctx = lax.rem(ctx + offset, ctx_count)
        return pltpu.make_async_remote_copy(
            src_ref=stage.at[:, pl.ds((pair * ctx_count + other_ctx) * 2 + first, count)],
            dst_ref=r_ref.at[:, pl.ds(2 * pair + first, count), my_block],
            send_sem=sent.at[1],
            recv_sem=got_s.at[2 * pair + first],
            device_id=(other_ctx, chan),
            device_id_type=MESH,
        )

    def columns(first, count):
        return pl.ds(first * lanes, count * lanes)

    def result_copy(pair, first, count, other):
        other_ctx, other_chan = other // chan_count, lax.rem(other, chan_count)
        return pltpu.make_async_remote_copy(
            src_ref=y_ref.at[pair, pl.ds(pl.multiple_of(other * rows, rows), rows), columns(first, count)],
            dst_ref=o_ref.at[slot(ctx, chan, pair), :, columns(first, count)],
            send_sem=sent.at[2],
            recv_sem=got_y.at[pair],
            device_id=(other_ctx, other_chan),
            device_id_type=MESH,
        )

    def settle(ref, sem):
        pltpu.make_async_copy(ref, ref, sem).wait()

    def turned(part, channel):
        flipped = s_ref[part * local_channels + channel].astype(jnp.bfloat16).T
        pieces = [flipped[f * block : (f + 1) * block] for f in range(flipped.shape[0] // block)]
        return jnp.concatenate(pieces, axis=1).astype(jnp.bfloat16)

    def turn(pair, begin, count):
        @pl.loop(1, ctx_count)
        def _(offset):
            first = (pair * ctx_count + lax.rem(ctx + offset, ctx_count)) * 2
            for part in range(2):
                for which in range(begin, begin + count):
                    stage[part, first + which] = turned(part, first + which)

    def turn_own(pair):
        for part in range(2):
            for which in range(2):
                r_ref[part, 2 * pair + which, my_block] = turned(part, (pair * ctx_count + ctx) * 2 + which)
        x_ref[pair, my_rows] = c_ref[slot(ctx, chan, pair)]

    def send_carried(pair):
        @pl.loop(1, total)
        def _(offset):
            carried_copy(pair, offset).start()

    def send_spectra(pair, first, count):
        @pl.loop(1, ctx_count)
        def _(offset):
            spectra_copy(pair, first, count, offset).start()

    chunk = 2 * lanes

    def forward(pair):
        settle(c_ref.at[pl.ds(0, total - 1)], got_c.at[pair])
        x = x_ref.at[pair]

        @pl.loop(0, rows_total // chunk)
        def _(step):
            at = pl.ds(pl.multiple_of(step * chunk, chunk), chunk)
            below = pl.ds(pl.multiple_of(rows_total + step * chunk, chunk), chunk)
            real, imag = dot(w1_ref[at], x[...]), dot(w1_ref[below], x[...])
            t_real, t_imag = tw_ref[0, at], tw_ref[1, at]
            for which in range(2):
                cols = slice(which * lanes, (which + 1) * lanes)
                a_real, a_imag = real[:, cols], imag[:, cols]
                twiddled = jnp.concatenate(
                    [a_real * t_real - a_imag * t_imag, a_real * t_imag + a_imag * t_real], axis=1
                )
                b_ref[2 * pair + which, at] = dot(twiddled.astype(jnp.bfloat16), w2_ref[...])

    def backward(pair, first, count):
        settle(stage.at[:, pl.ds(0, count * (ctx_count - 1))], got_s.at[2 * pair + first])

        @pl.loop(0, rows_total // chunk)
        def _(step):
            at = pl.ds(pl.multiple_of(step * chunk, chunk), chunk)
            below = pl.ds(pl.multiple_of(rows_total + step * chunk, chunk), chunk)
            t_real, t_imag = tw_ref[0, at], tw_ref[1, at]
            for which in range(first, first + count):
                cols = slice(which * lanes, (which + 1) * lanes)
                bins = b_ref[2 * pair + which, at]
                b_real, b_imag = bins[:, :lanes], bins[:, lanes:]
                f_real = r_ref[0, 2 * pair + which, at].astype(jnp.float32)
                f_imag = r_ref[1, 2 * pair + which, at].astype(jnp.float32)
                shaped = jnp.concatenate(
                    [b_real * f_real - b_imag * f_imag, b_real * f_imag + b_imag * f_real], axis=1
                )
                back = dot(shaped.astype(jnp.bfloat16), w3_ref[...])
                z_real, z_imag = back[:, :lanes], back[:, lanes:]
                g_ref[at, cols] = (z_real * t_real + z_imag * t_imag).astype(jnp.bfloat16)
                g_ref[below, cols] = (z_imag * t_real - z_real * t_imag).astype(jnp.bfloat16)

        steps = rows_total // chunk
        spread = total // steps
        home = me // spread
        cols = slice(first * lanes, (first + count) * lanes)

        @pl.loop(0, steps)
        def _(step):
            turn_of = lax.rem(home + 1 + step, steps)
            at = pl.ds(pl.multiple_of(turn_of * chunk, chunk), chunk)
            y_ref[pair, at, cols] = dot(v1_ref[at], g_ref[:, cols]).astype(jnp.bfloat16)

            @pl.loop(0, spread)
            def _(index):
                other = turn_of * spread + lax.rem(me + 1 + index, spread)

                @pl.when(other != me)
                def _():
                    result_copy(pair, first, count, other).start()

        o_ref[slot(ctx, chan, pair), :, cols] = y_ref[pair, my_rows, cols]

    def finish(pair):
        settle(o_ref.at[pl.ds(0, total - 1)], got_y.at[pair])

        @pl.loop(0, chan_count)
        def _(chan_index):
            first = slot(0, chan_index, pair)
            sums = []
            for i in range(ctx_count):
                for which in range(2):
                    cols = slice(which * lanes, (which + 1) * lanes)
                    carried = c_ref[first + i, :, cols].astype(jnp.float32)
                    gain = skip_ref[2 * (first + i) + which]
                    sums.append(o_ref[first + i, :, cols].astype(jnp.float32) + gain * carried)
            flat = jnp.stack(sums).reshape(group, rows * lanes)
            at = pl.ds(pl.multiple_of(first * 2, group), group)
            out_ref[at] = (gate_ref[at].astype(jnp.float32) * flat).astype(jnp.bfloat16)

    def meet_plane():
        @pl.when(even)
        def _():
            pl.semaphore_wait(barrier, ctx_count - 1)
            signal(ready, partner)

        @pl.when(jnp.logical_not(even))
        def _():
            pl.semaphore_wait(ready, 1)

    def meet_all():
        @pl.when(jnp.logical_not(even))
        def _():
            pl.semaphore_wait(barrier, ctx_count * (chan_count - 1))
            signal(ready, partner)

        @pl.when(even)
        def _():
            pl.semaphore_wait(ready, 1)

    waited = set()

    def need(*indices):
        for index in indices:
            if index not in waited:
                waited.add(index)
                loads[index].wait()

    need(0, 1)
    pack(0)
    need(0, 1)
    pack(1)
    need(0, 1)
    pack(2)
    meet_plane()
    meet_all()
    send_carried(0)
    send_carried(1)
    send_carried(2)
    need(2, 11)
    turn(0, 0, 1)
    send_spectra(0, 0, 1)
    need(2, 11)
    turn(0, 1, 1)
    send_spectra(0, 1, 1)
    need(12, 13)
    turn(1, 0, 2)
    send_spectra(1, 0, 2)
    need(12, 13)
    turn(2, 0, 2)
    send_spectra(2, 0, 1)
    send_spectra(2, 1, 1)
    need(2, 11)
    turn_own(0)
    need(12, 13)
    turn_own(1)
    need(12, 13)
    turn_own(2)
    need(3, 4, 6)
    forward(0)
    need(5, 7, 8)
    backward(0, 0, 1)
    need(3, 4, 6)
    forward(1)
    need(5, 7, 8)
    backward(0, 1, 1)
    need(5, 7, 8)
    backward(1, 0, 2)
    need(3, 4, 6)
    forward(2)
    need(5, 7, 8)
    backward(2, 0, 1)
    need(5, 7, 8)
    backward(2, 1, 1)
    need(9, 10)
    finish(0)
    need(9, 10)
    finish(1)
    need(9, 10)
    finish(2)
    settle(c_ref.at[pl.ds(0, pairs * (total - 1))], sent.at[0])
    settle(stage.at[:, pl.ds(0, 2 * pairs * (ctx_count - 1))], sent.at[1])
    settle(o_ref.at[pl.ds(0, pairs * (total - 1))], sent.at[2])


def channel_body(value_branch, key_branch, gate_branch, skip_gain, spectra):
    channels, tokens = value_branch.shape
    ctx_count, chan_count = lax.axis_size("ctx"), lax.axis_size("chan")
    total = ctx_count * chan_count
    rows = tokens // lanes
    rows_total = rows * total
    pairs = channels // total // 2
    local_channels = spectra.shape[1]
    block = spectra.shape[3] // lanes
    table, turns = [jnp.asarray(t) for t in transform_tables(rows_total, ctx_count, 2 * channels * tokens)]
    sems = lambda *shape: pltpu.SemaphoreType.DMA(shape)
    hbm = pl.BlockSpec(memory_space=pl.ANY)
    packed = pltpu.VMEM((channels // 2, rows, 2 * lanes), jnp.bfloat16)
    held = pltpu.VMEM((channels, tokens), jnp.bfloat16)
    half = lambda *shape: pltpu.VMEM(shape, jnp.bfloat16)
    return pl.pallas_call(
        functools.partial(fused_kernel, ctx_count, chan_count),
        in_specs=[hbm] * 7,
        out_specs=VMEM,
        out_shape=jax.ShapeDtypeStruct((channels, tokens), jnp.bfloat16),
        scratch_shapes=[
            pltpu.SMEM((channels,), jnp.float32),
            half(2 * rows_total, rows_total),
            half(2 * lanes, 2 * lanes),
            half(2 * lanes, 2 * lanes),
            half(rows_total, 2 * rows_total),
            pltpu.VMEM((2, rows_total, lanes), jnp.float32),
            pltpu.VMEM((2 * local_channels, block, lanes), jnp.float32),
            half(2, local_channels, block, lanes),
            half(2, 2 * pairs, rows_total, lanes),
            half(pairs, rows_total, 2 * lanes),
            half(pairs, rows_total, 2 * lanes),
            half(2 * rows_total, 2 * lanes),
            pltpu.VMEM((2 * pairs, rows_total, 2 * lanes), jnp.float32),
            held, held, held, packed, packed,
            sems(3), sems(pairs), sems(2 * pairs), sems(pairs), sems(14), pltpu.SemaphoreType.REGULAR,
        ],
        compiler_params=pltpu.CompilerParams(collective_id=0, has_side_effects=True, vmem_limit_bytes=55369728),
    )(
        pltpu.with_memory_space_constraint(skip_gain, pltpu.HBM),
        value_branch,
        key_branch,
        gate_branch,
        spectra.reshape(2 * local_channels, block, lanes),
        table,
        turns,
    )


def body(value_branch, key_branch, gate_branch, skip_gain, spectra):
    channels, tokens = value_branch.shape
    ctx_count, chan_count = lax.axis_size("ctx"), lax.axis_size("chan")
    total = ctx_count * chan_count
    block_rows = tokens * chan_count // lanes
    fits = (
        channels % (2 * total) == 0
        and ctx_count % 8 == 0
        and tokens % (16 * lanes) == 0
        and block_rows <= lanes
        and lanes % block_rows == 0
        and (tokens * total // lanes) % lanes == 0
    )
    chosen = channel_body if fits else blockwise_body
    return chosen(value_branch, key_branch, gate_branch, skip_gain, spectra)


def solution(mesh):
    in_specs = (
        P(None, ("ctx", "chan")),
        P(None, ("ctx", "chan")),
        P(None, ("ctx", "chan")),
        P(),
        P(None, "chan", "ctx", None),
    )
    out_specs = P(None, ("ctx", "chan"))
    return jax.shard_map(body, mesh=mesh, in_specs=in_specs, out_specs=out_specs, check_vma=False)
```

```python
import functools
import math

import jax
import jax.numpy as jnp
import numpy as np
from jax import lax
from jax.experimental import pallas as pl
from jax.experimental.pallas import tpu as pltpu
from jax.sharding import PartitionSpec as P

two_pi = 2.0 * math.pi
first_factor = 128
highest = lax.Precision.HIGHEST


def reversed_bits(numbers, bit_count):
    result = numbers * 0
    for bit_number in range(bit_count):
        result = result + (numbers >> bit_number & 1) * (1 << bit_count - 1 - bit_number)
    return result


def phase_pair(radians):
    return (jnp.cos(radians), jnp.sin(radians))


def block_table(length_of, direction):
    counter = jnp.arange(length_of, dtype=jnp.int32)
    product = counter[:, None] * counter[None, :] % length_of
    cosine, sine = phase_pair(direction * two_pi / length_of * product.astype(jnp.float32))
    upper_rows = jnp.stack([cosine, -sine], axis=1)
    lower_rows = jnp.stack([sine, cosine], axis=1)
    return jnp.stack([upper_rows, lower_rows], axis=0)


def complex_mul(signal, factor):
    factor_real, factor_imag = factor
    return jnp.stack(
        [
            signal[0] * factor_real - signal[1] * factor_imag,
            signal[0] * factor_imag + signal[1] * factor_real,
        ]
    )


def forward_local(signal):
    channel_count, seq_length = (signal.shape[1], signal.shape[2])
    second_factor = seq_length // first_factor
    blocked = signal.reshape(2, channel_count, first_factor, second_factor)
    section_one = jnp.einsum(
        "orca,cxaq->oxrq", block_table(first_factor, -1.0), blocked, precision=highest
    )
    column = jnp.arange(first_factor, dtype=jnp.int32)[:, None]
    within = jnp.arange(second_factor, dtype=jnp.int32)[None, :]
    twiddle = phase_pair(-two_pi / seq_length * (column * within).astype(jnp.float32))
    section_two = complex_mul(section_one, twiddle)
    section_three = jnp.einsum(
        "peoq,oxrq->pxer", block_table(second_factor, -1.0), section_two, precision=highest
    )
    return section_three.reshape(2, channel_count, seq_length)


def inverse_local(signal):
    channel_count, seq_length = (signal.shape[1], signal.shape[2])
    second_factor = seq_length // first_factor
    blocked = signal.reshape(2, channel_count, second_factor, first_factor)
    section_one = jnp.einsum(
        "pqoe,oxer->pxqr", block_table(second_factor, 1.0), blocked, precision=highest
    )
    within = jnp.arange(second_factor, dtype=jnp.int32)[:, None]
    column = jnp.arange(first_factor, dtype=jnp.int32)[None, :]
    twiddle = phase_pair(two_pi / seq_length * (within * column).astype(jnp.float32))
    section_two = complex_mul(section_one, twiddle)
    section_three = jnp.einsum(
        "paor,oxqr->pxaq", block_table(first_factor, 1.0), section_two, precision=highest
    )
    return section_three.reshape(2, channel_count, seq_length)


def blockwise_body(value_branch, key_branch, gate_branch, skip_gain, spectra):
    carried = (key_branch.astype(jnp.float32) * value_branch.astype(jnp.float32)).astype(
        jnp.bfloat16
    )
    series = lax.all_to_all(carried, "chan", split_axis=0, concat_axis=1, tiled=True)
    channel_count, seq_length = series.shape
    ctx_count = lax.axis_size("ctx")
    bit_count = ctx_count.bit_length() - 1
    device = lax.axis_index("ctx")
    total_length = seq_length * ctx_count
    counter = jnp.arange(ctx_count, dtype=jnp.int32)
    target = reversed_bits(counter, bit_count)
    blocks = lax.all_to_all(
        series.reshape(channel_count, 1, seq_length), "ctx", split_axis=2, concat_axis=1, tiled=True
    )
    matrix = jnp.stack(
        phase_pair(
            -two_pi
            / ctx_count
            * (target[:, None] * counter[None, :] % ctx_count).astype(jnp.float32)
        )
    )
    rows = jnp.einsum("ojp,xps->oxjs", matrix, blocks.astype(jnp.float32), precision=highest)
    received = lax.all_to_all(rows, "ctx", split_axis=2, concat_axis=3, tiled=True)
    signal = received.reshape(2, channel_count, seq_length)
    device_rank = reversed_bits(device, bit_count)
    positions = jnp.arange(seq_length, dtype=jnp.int32)
    radians = two_pi / total_length * (positions * device_rank).astype(jnp.float32)
    signal = complex_mul(signal, phase_pair(-radians))
    spectrum = forward_local(signal)
    shaped = complex_mul(spectrum, (spectra[0, :, 0, :], spectra[1, :, 0, :]))
    returned = complex_mul(inverse_local(shaped), phase_pair(radians))
    parts = lax.all_to_all(
        returned.reshape(2, channel_count, 1, seq_length),
        "ctx",
        split_axis=3,
        concat_axis=2,
        tiled=True,
    )
    cosine, sine = phase_pair(
        two_pi / ctx_count * (counter[:, None] * target[None, :] % ctx_count).astype(jnp.float32)
    )
    matrix = jnp.stack([cosine, -sine])
    summed = jnp.einsum("opj,oxjs->xps", matrix, parts, precision=highest) / total_length
    local_conv = summed.astype(jnp.bfloat16)
    convolved = lax.all_to_all(local_conv, "ctx", split_axis=1, concat_axis=2, tiled=True).reshape(
        channel_count, seq_length
    )
    tokens_conv = lax.all_to_all(convolved, "chan", split_axis=1, concat_axis=0, tiled=True)
    result = gate_branch.astype(jnp.float32) * (
        tokens_conv.astype(jnp.float32) + skip_gain[:, None] * carried.astype(jnp.float32)
    )
    return result.astype(jnp.bfloat16)


lanes = 128
MESH = pl.DeviceIdType.MESH
VMEM = pl.BlockSpec(memory_space=pltpu.VMEM)


@functools.lru_cache(maxsize=None)
def transform_tables(rows_total, ctx_count, least_bytes):
    length = rows_total * lanes
    bit_count = ctx_count.bit_length() - 1
    rev = np.array([int(format(j, "b").zfill(bit_count)[::-1], 2) if bit_count else 0 for j in range(ctx_count)])
    a = np.arange(rows_total // ctx_count)
    k1 = (rev[:, None] + ctx_count * a[None, :]).reshape(-1)
    fold = lanes // (rows_total // ctx_count)
    k2 = np.arange(lanes).reshape(lanes // fold, fold).T.reshape(-1)
    n1, n2 = np.arange(rows_total), np.arange(lanes)
    f1 = np.exp(-2j * np.pi * (np.outer(k1, n1) % rows_total) / rows_total)
    f2 = np.exp(-2j * np.pi * (np.outer(n2, k2) % lanes) / lanes)
    tw = np.exp(-2j * np.pi * (np.outer(k1, n2) % length) / length)
    w1 = np.stack([f1.real, f1.imag])
    w2 = np.block([[f2.real, f2.imag], [-f2.imag, f2.real]])
    b2 = f2.conj().T
    w3 = np.block([[b2.real, b2.imag], [-b2.imag, b2.real]])
    b1 = f1.conj().T / length
    v1 = np.concatenate([b1.real, -b1.imag], axis=1)
    half = lambda t: np.asarray(t, dtype=jnp.bfloat16)
    pieces = [w1.reshape(2 * rows_total, rows_total), v1[:, :rows_total], v1[:, rows_total:]]
    square = np.concatenate([w2, w3], axis=1)
    pieces.append(np.pad(square, ((0, 0), (0, max(rows_total - square.shape[1], 0)))))
    turns = np.stack([tw.real, tw.imag]).astype(np.float32)
    spare = np.zeros((2 * (least_bytes // turns.nbytes),) + turns.shape[1:], np.float32)
    return np.concatenate(pieces).astype(jnp.bfloat16), np.concatenate([turns, spare])


def wrap(number, count):
    return number & (count - 1) if count & (count - 1) == 0 else lax.rem(number, count)


def over(number, count):
    return number >> (count.bit_length() - 1) if count & (count - 1) == 0 else number // count


def dot(a, b):
    return jnp.dot(a, b, preferred_element_type=jnp.float32)


def fused_kernel(ctx_count, chan_count, skip_hbm, v_hbm, k_hbm, gate_hbm, s_hbm, table_hbm, tw_hbm, out_ref, *refs):
    skip_ref, w1_ref, w2_ref, w3_ref, v1_ref, tw_ref = refs[:6]
    s_ref, stage, r_ref, x_ref, y_ref, g_ref, b_ref = refs[6:13]
    v_ref, k_ref, gate_ref, c_ref, o_ref = refs[13:18]
    sent, got_c, got_s, got_y, local, ready = refs[18:]
    ctx, chan = lax.axis_index("ctx"), lax.axis_index("chan")
    me = ctx * chan_count + chan
    total = ctx_count * chan_count
    pairs, rows = x_ref.shape[0], c_ref.shape[1]
    rows_total = x_ref.shape[1]
    block = stage.shape[2]
    local_channels = stage.shape[1]
    wide = 2 * lanes

    def load(index, source, target):
        return pltpu.make_async_copy(source, target, local.at[index])

    first_rows = 2 * rows_total
    share = 2 * ctx_count
    rest = local_channels - share
    loads = [
        load(0, v_hbm, v_ref),
        load(1, k_hbm, k_ref),
        load(2, s_hbm.at[pl.ds(0, share)], s_ref.at[pl.ds(0, share)]),
        load(3, table_hbm.at[pl.ds(0, first_rows)], w1_ref),
        load(4, table_hbm.at[pl.ds(2 * first_rows, wide), pl.ds(0, wide)], w2_ref),
        load(5, table_hbm.at[pl.ds(2 * first_rows, wide), pl.ds(wide, wide)], w3_ref),
        load(6, tw_hbm.at[pl.ds(0, 2)], tw_ref),
        load(7, table_hbm.at[pl.ds(first_rows, rows_total)], v1_ref.at[:, pl.ds(0, rows_total)]),
        load(8, table_hbm.at[pl.ds(first_rows + rows_total, rows_total)], v1_ref.at[:, pl.ds(rows_total, rows_total)]),
        load(9, gate_hbm, gate_ref),
        load(10, skip_hbm, skip_ref),
        load(11, s_hbm.at[pl.ds(local_channels, share)], s_ref.at[pl.ds(local_channels, share)]),
        load(12, s_hbm.at[pl.ds(share, rest)], s_ref.at[pl.ds(share, rest)]),
        load(13, s_hbm.at[pl.ds(local_channels + share, rest)], s_ref.at[pl.ds(local_channels + share, rest)]),
    ]
    barrier = pltpu.get_barrier_semaphore()
    even = lax.rem(ctx, 2) == 0
    partner = (ctx + 1 - 2 * lax.rem(ctx, 2), chan)

    def signal(semaphore, device):
        pl.semaphore_signal(semaphore, inc=1, device_id=device, device_id_type=MESH)

    for index in (0, 1, 2, 11):
        loads[index].start()

    @pl.loop(0, ctx_count // 2)
    def _(chip):
        @pl.when(2 * chip != ctx)
        def _():
            signal(barrier, (2 * chip, chan))

        @pl.loop(1, chan_count)
        def _(offset):
            signal(barrier, (2 * chip + 1, lax.rem(chan + offset, chan_count)))

    for index in (12, 13, 3, 4, 6, 5, 7, 8, 9, 10):
        loads[index].start()
    group = 2 * ctx_count

    def pack(pair):
        @pl.loop(0, chan_count)
        def _(chan_index):
            index = chan_index * pairs + pair
            at = pl.ds(pl.multiple_of(index * group, group), group)
            product = (k_ref[at].astype(jnp.float32) * v_ref[at].astype(jnp.float32)).astype(jnp.bfloat16)
            split = product.astype(jnp.float32).reshape(ctx_count, 2, rows, lanes)
            packed = jnp.concatenate([split[:, 0], split[:, 1]], axis=2)
            c_ref[pl.ds(index * ctx_count, ctx_count)] = packed.astype(jnp.bfloat16)

    def place(offset):
        other = wrap(me + offset, total)
        return other, over(other, chan_count), wrap(other, chan_count)

    def slot(ctx_index, chan_index, pair):
        return (chan_index * pairs + pair) * ctx_count + ctx_index

    my_rows = pl.ds(pl.multiple_of(me * rows, rows), rows)
    my_block = pl.ds(pl.multiple_of(ctx * block, block), block)

    def carried_copy(pair, offset):
        other, other_ctx, other_chan = place(offset)
        return pltpu.make_async_remote_copy(
            src_ref=c_ref.at[slot(other_ctx, other_chan, pair)],
            dst_ref=x_ref.at[pair, my_rows],
            send_sem=sent.at[0],
            recv_sem=got_c.at[pair],
            device_id=(other_ctx, other_chan),
            device_id_type=MESH,
        )

    def spectra_copy(pair, first, count, offset):
        other_ctx = wrap(ctx + offset, ctx_count)
        return pltpu.make_async_remote_copy(
            src_ref=stage.at[:, pl.ds((pair * ctx_count + other_ctx) * 2 + first, count)],
            dst_ref=r_ref.at[:, pl.ds(2 * pair + first, count), my_block],
            send_sem=sent.at[1],
            recv_sem=got_s.at[2 * pair + first],
            device_id=(other_ctx, chan),
            device_id_type=MESH,
        )

    def columns(first, count):
        return pl.ds(first * lanes, count * lanes)

    def result_copy(pair, first, count, other):
        other_ctx, other_chan = over(other, chan_count), wrap(other, chan_count)
        return pltpu.make_async_remote_copy(
            src_ref=y_ref.at[pair, pl.ds(pl.multiple_of(other * rows, rows), rows), columns(first, count)],
            dst_ref=o_ref.at[slot(ctx, chan, pair), :, columns(first, count)],
            send_sem=sent.at[2],
            recv_sem=got_y.at[pair, chan],
            device_id=(other_ctx, other_chan),
            device_id_type=MESH,
        )

    def settle(ref, sem):
        pltpu.make_async_copy(ref, ref, sem).wait()

    def turned(part, channel):
        flipped = s_ref[part * local_channels + channel].astype(jnp.bfloat16).T
        pieces = [flipped[f * block : (f + 1) * block] for f in range(flipped.shape[0] // block)]
        return jnp.concatenate(pieces, axis=1).astype(jnp.bfloat16)

    def turn(pair, begin, count):
        @pl.loop(1, ctx_count)
        def _(offset):
            first = (pair * ctx_count + lax.rem(ctx + offset, ctx_count)) * 2
            for part in range(2):
                for which in range(begin, begin + count):
                    stage[part, first + which] = turned(part, first + which)

    def turn_own(pair):
        for part in range(2):
            for which in range(2):
                r_ref[part, 2 * pair + which, my_block] = turned(part, (pair * ctx_count + ctx) * 2 + which)
        x_ref[pair, my_rows] = c_ref[slot(ctx, chan, pair)]

    def send_carried(pair):
        @pl.loop(1, total)
        def _(offset):
            carried_copy(pair, offset).start()

    def send_spectra(pair, first, count):
        @pl.loop(1, ctx_count)
        def _(offset):
            spectra_copy(pair, first, count, offset).start()

    chunk = 2 * lanes

    def forward(pair):
        settle(c_ref.at[pl.ds(0, total - 1)], got_c.at[pair])
        x = x_ref.at[pair]

        @pl.loop(0, rows_total // chunk)
        def _(step):
            at = pl.ds(pl.multiple_of(step * chunk, chunk), chunk)
            below = pl.ds(pl.multiple_of(rows_total + step * chunk, chunk), chunk)
            real, imag = dot(w1_ref[at], x[...]), dot(w1_ref[below], x[...])
            t_real, t_imag = tw_ref[0, at], tw_ref[1, at]
            for which in range(2):
                cols = slice(which * lanes, (which + 1) * lanes)
                a_real, a_imag = real[:, cols], imag[:, cols]
                twiddled = jnp.concatenate(
                    [a_real * t_real - a_imag * t_imag, a_real * t_imag + a_imag * t_real], axis=1
                )
                b_ref[2 * pair + which, at] = dot(twiddled.astype(jnp.bfloat16), w2_ref[...])

    def backward(pair, first, count):
        settle(stage.at[:, pl.ds(0, count * (ctx_count - 1))], got_s.at[2 * pair + first])

        @pl.loop(0, rows_total // chunk)
        def _(step):
            at = pl.ds(pl.multiple_of(step * chunk, chunk), chunk)
            below = pl.ds(pl.multiple_of(rows_total + step * chunk, chunk), chunk)
            t_real, t_imag = tw_ref[0, at], tw_ref[1, at]
            for which in range(first, first + count):
                cols = slice(which * lanes, (which + 1) * lanes)
                bins = b_ref[2 * pair + which, at]
                b_real, b_imag = bins[:, :lanes], bins[:, lanes:]
                f_real = r_ref[0, 2 * pair + which, at].astype(jnp.float32)
                f_imag = r_ref[1, 2 * pair + which, at].astype(jnp.float32)
                shaped = jnp.concatenate(
                    [b_real * f_real - b_imag * f_imag, b_real * f_imag + b_imag * f_real], axis=1
                )
                back = dot(shaped.astype(jnp.bfloat16), w3_ref[...])
                z_real, z_imag = back[:, :lanes], back[:, lanes:]
                g_ref[at, cols] = (z_real * t_real + z_imag * t_imag).astype(jnp.bfloat16)
                g_ref[below, cols] = (z_imag * t_real - z_real * t_imag).astype(jnp.bfloat16)

        steps = rows_total // chunk
        spread = total // steps
        home = me // spread
        cols = slice(first * lanes, (first + count) * lanes)

        @pl.loop(0, steps)
        def _(step):
            turn_of = lax.rem(home + 1 + step, steps)
            at = pl.ds(pl.multiple_of(turn_of * chunk, chunk), chunk)
            y_ref[pair, at, cols] = dot(v1_ref[at], g_ref[:, cols]).astype(jnp.bfloat16)

            @pl.loop(0, spread)
            def _(index):
                other = turn_of * spread + wrap(me + 1 + index, spread)

                @pl.when(other != me)
                def _():
                    result_copy(pair, first, count, other).start()

        o_ref[slot(ctx, chan, pair), :, cols] = y_ref[pair, my_rows, cols]

    def finish(pair):
        settle(o_ref.at[pl.ds(0, ctx_count - 1)], got_y.at[pair, chan])
        gate_group(pair, chan)

        @pl.loop(1, chan_count)
        def _(offset):
            chan_index = lax.rem(chan + offset, chan_count)
            settle(o_ref.at[pl.ds(0, ctx_count)], got_y.at[pair, chan_index])
            gate_group(pair, chan_index)

    def gate_group(pair, chan_index):
        first = slot(0, chan_index, pair)
        sums = []
        for i in range(ctx_count):
            for which in range(2):
                cols = slice(which * lanes, (which + 1) * lanes)
                carried = c_ref[first + i, :, cols].astype(jnp.float32)
                gain = skip_ref[2 * (first + i) + which]
                sums.append(o_ref[first + i, :, cols].astype(jnp.float32) + gain * carried)
        flat = jnp.stack(sums).reshape(group, rows * lanes)
        at = pl.ds(pl.multiple_of(first * 2, group), group)
        out_ref[at] = (gate_ref[at].astype(jnp.float32) * flat).astype(jnp.bfloat16)

    def meet_plane():
        @pl.when(even)
        def _():
            pl.semaphore_wait(barrier, ctx_count - 1)
            signal(ready, partner)

        @pl.when(jnp.logical_not(even))
        def _():
            pl.semaphore_wait(ready, 1)

    def meet_all():
        @pl.when(jnp.logical_not(even))
        def _():
            pl.semaphore_wait(barrier, ctx_count * (chan_count - 1))
            signal(ready, partner)

        @pl.when(even)
        def _():
            pl.semaphore_wait(ready, 1)

    waited = set()

    def need(*indices):
        for index in indices:
            if index not in waited:
                waited.add(index)
                loads[index].wait()

    need(0, 1)
    pack(0)
    need(0, 1)
    pack(1)
    need(0, 1)
    pack(2)
    meet_plane()
    meet_all()
    send_carried(0)
    send_carried(1)
    send_carried(2)
    need(2, 11)
    turn(0, 0, 1)
    send_spectra(0, 0, 1)
    need(2, 11)
    turn(0, 1, 1)
    send_spectra(0, 1, 1)
    need(12, 13)
    turn(1, 0, 1)
    send_spectra(1, 0, 1)
    need(12, 13)
    turn(1, 1, 1)
    send_spectra(1, 1, 1)
    need(12, 13)
    turn(2, 0, 2)
    send_spectra(2, 0, 1)
    send_spectra(2, 1, 1)
    need(2, 11)
    turn_own(0)
    need(3, 4, 6)
    forward(0)
    need(5, 7, 8)
    backward(0, 0, 1)
    need(12, 13)
    turn_own(1)
    need(3, 4, 6)
    forward(1)
    need(5, 7, 8)
    backward(0, 1, 1)
    need(5, 7, 8)
    backward(1, 0, 1)
    need(12, 13)
    turn_own(2)
    need(3, 4, 6)
    forward(2)
    need(5, 7, 8)
    backward(1, 1, 1)
    need(5, 7, 8)
    backward(2, 0, 1)
    need(5, 7, 8)
    backward(2, 1, 1)
    need(9, 10)
    finish(0)
    need(9, 10)
    finish(1)
    need(9, 10)
    finish(2)
    settle(c_ref.at[pl.ds(0, pairs * (total - 1))], sent.at[0])
    settle(stage.at[:, pl.ds(0, 2 * pairs * (ctx_count - 1))], sent.at[1])
    settle(o_ref.at[pl.ds(0, pairs * (total - 1))], sent.at[2])


def channel_body(value_branch, key_branch, gate_branch, skip_gain, spectra):
    channels, tokens = value_branch.shape
    ctx_count, chan_count = lax.axis_size("ctx"), lax.axis_size("chan")
    total = ctx_count * chan_count
    rows = tokens // lanes
    rows_total = rows * total
    pairs = channels // total // 2
    local_channels = spectra.shape[1]
    block = spectra.shape[3] // lanes
    table, turns = [jnp.asarray(t) for t in transform_tables(rows_total, ctx_count, 2 * channels * tokens)]
    sems = lambda *shape: pltpu.SemaphoreType.DMA(shape)
    hbm = pl.BlockSpec(memory_space=pl.ANY)
    packed = pltpu.VMEM((channels // 2, rows, 2 * lanes), jnp.bfloat16)
    held = pltpu.VMEM((channels, tokens), jnp.bfloat16)
    half = lambda *shape: pltpu.VMEM(shape, jnp.bfloat16)
    return pl.pallas_call(
        functools.partial(fused_kernel, ctx_count, chan_count),
        in_specs=[hbm] * 7,
        out_specs=VMEM,
        out_shape=jax.ShapeDtypeStruct((channels, tokens), jnp.bfloat16),
        scratch_shapes=[
            pltpu.SMEM((channels,), jnp.float32),
            half(2 * rows_total, rows_total),
            half(2 * lanes, 2 * lanes),
            half(2 * lanes, 2 * lanes),
            half(rows_total, 2 * rows_total),
            pltpu.VMEM((2, rows_total, lanes), jnp.float32),
            pltpu.VMEM((2 * local_channels, block, lanes), jnp.float32),
            half(2, local_channels, block, lanes),
            half(2, 2 * pairs, rows_total, lanes),
            half(pairs, rows_total, 2 * lanes),
            half(pairs, rows_total, 2 * lanes),
            half(2 * rows_total, 2 * lanes),
            pltpu.VMEM((2 * pairs, rows_total, 2 * lanes), jnp.float32),
            held, held, held, packed, packed,
            sems(3), sems(pairs), sems(2 * pairs), sems(pairs, chan_count), sems(14), pltpu.SemaphoreType.REGULAR,
        ],
        compiler_params=pltpu.CompilerParams(collective_id=0, has_side_effects=True, vmem_limit_bytes=55369728),
    )(
        pltpu.with_memory_space_constraint(skip_gain, pltpu.HBM),
        value_branch,
        key_branch,
        gate_branch,
        spectra.reshape(2 * local_channels, block, lanes),
        table,
        turns,
    )


def body(value_branch, key_branch, gate_branch, skip_gain, spectra):
    channels, tokens = value_branch.shape
    ctx_count, chan_count = lax.axis_size("ctx"), lax.axis_size("chan")
    total = ctx_count * chan_count
    block_rows = tokens * chan_count // lanes
    fits = (
        channels % (2 * total) == 0
        and ctx_count % 8 == 0
        and tokens % (16 * lanes) == 0
        and block_rows <= lanes
        and lanes % block_rows == 0
        and (tokens * total // lanes) % lanes == 0
    )
    chosen = channel_body if fits else blockwise_body
    return chosen(value_branch, key_branch, gate_branch, skip_gain, spectra)


def solution(mesh):
    in_specs = (
        P(None, ("ctx", "chan")),
        P(None, ("ctx", "chan")),
        P(None, ("ctx", "chan")),
        P(),
        P(None, "chan", "ctx", None),
    )
    out_specs = P(None, ("ctx", "chan"))
    return jax.shard_map(body, mesh=mesh, in_specs=in_specs, out_specs=out_specs, check_vma=False)
```

```python
import functools
import math

import jax
import jax.numpy as jnp
import numpy as np
from jax import lax
from jax.experimental import pallas as pl
from jax.experimental.pallas import tpu as pltpu
from jax.sharding import PartitionSpec as P

two_pi = 2.0 * math.pi
first_factor = 128
highest = lax.Precision.HIGHEST


def reversed_bits(numbers, bit_count):
    result = numbers * 0
    for bit_number in range(bit_count):
        result = result + (numbers >> bit_number & 1) * (1 << bit_count - 1 - bit_number)
    return result


def phase_pair(radians):
    return (jnp.cos(radians), jnp.sin(radians))


def block_table(length_of, direction):
    counter = jnp.arange(length_of, dtype=jnp.int32)
    product = counter[:, None] * counter[None, :] % length_of
    cosine, sine = phase_pair(direction * two_pi / length_of * product.astype(jnp.float32))
    upper_rows = jnp.stack([cosine, -sine], axis=1)
    lower_rows = jnp.stack([sine, cosine], axis=1)
    return jnp.stack([upper_rows, lower_rows], axis=0)


def complex_mul(signal, factor):
    factor_real, factor_imag = factor
    return jnp.stack(
        [
            signal[0] * factor_real - signal[1] * factor_imag,
            signal[0] * factor_imag + signal[1] * factor_real,
        ]
    )


def forward_local(signal):
    channel_count, seq_length = (signal.shape[1], signal.shape[2])
    second_factor = seq_length // first_factor
    blocked = signal.reshape(2, channel_count, first_factor, second_factor)
    section_one = jnp.einsum(
        "orca,cxaq->oxrq", block_table(first_factor, -1.0), blocked, precision=highest
    )
    column = jnp.arange(first_factor, dtype=jnp.int32)[:, None]
    within = jnp.arange(second_factor, dtype=jnp.int32)[None, :]
    twiddle = phase_pair(-two_pi / seq_length * (column * within).astype(jnp.float32))
    section_two = complex_mul(section_one, twiddle)
    section_three = jnp.einsum(
        "peoq,oxrq->pxer", block_table(second_factor, -1.0), section_two, precision=highest
    )
    return section_three.reshape(2, channel_count, seq_length)


def inverse_local(signal):
    channel_count, seq_length = (signal.shape[1], signal.shape[2])
    second_factor = seq_length // first_factor
    blocked = signal.reshape(2, channel_count, second_factor, first_factor)
    section_one = jnp.einsum(
        "pqoe,oxer->pxqr", block_table(second_factor, 1.0), blocked, precision=highest
    )
    within = jnp.arange(second_factor, dtype=jnp.int32)[:, None]
    column = jnp.arange(first_factor, dtype=jnp.int32)[None, :]
    twiddle = phase_pair(two_pi / seq_length * (within * column).astype(jnp.float32))
    section_two = complex_mul(section_one, twiddle)
    section_three = jnp.einsum(
        "paor,oxqr->pxaq", block_table(first_factor, 1.0), section_two, precision=highest
    )
    return section_three.reshape(2, channel_count, seq_length)


def blockwise_body(value_branch, key_branch, gate_branch, skip_gain, spectra):
    carried = (key_branch.astype(jnp.float32) * value_branch.astype(jnp.float32)).astype(
        jnp.bfloat16
    )
    series = lax.all_to_all(carried, "chan", split_axis=0, concat_axis=1, tiled=True)
    channel_count, seq_length = series.shape
    ctx_count = lax.axis_size("ctx")
    bit_count = ctx_count.bit_length() - 1
    device = lax.axis_index("ctx")
    total_length = seq_length * ctx_count
    counter = jnp.arange(ctx_count, dtype=jnp.int32)
    target = reversed_bits(counter, bit_count)
    blocks = lax.all_to_all(
        series.reshape(channel_count, 1, seq_length), "ctx", split_axis=2, concat_axis=1, tiled=True
    )
    matrix = jnp.stack(
        phase_pair(
            -two_pi
            / ctx_count
            * (target[:, None] * counter[None, :] % ctx_count).astype(jnp.float32)
        )
    )
    rows = jnp.einsum("ojp,xps->oxjs", matrix, blocks.astype(jnp.float32), precision=highest)
    received = lax.all_to_all(rows, "ctx", split_axis=2, concat_axis=3, tiled=True)
    signal = received.reshape(2, channel_count, seq_length)
    device_rank = reversed_bits(device, bit_count)
    positions = jnp.arange(seq_length, dtype=jnp.int32)
    radians = two_pi / total_length * (positions * device_rank).astype(jnp.float32)
    signal = complex_mul(signal, phase_pair(-radians))
    spectrum = forward_local(signal)
    shaped = complex_mul(spectrum, (spectra[0, :, 0, :], spectra[1, :, 0, :]))
    returned = complex_mul(inverse_local(shaped), phase_pair(radians))
    parts = lax.all_to_all(
        returned.reshape(2, channel_count, 1, seq_length),
        "ctx",
        split_axis=3,
        concat_axis=2,
        tiled=True,
    )
    cosine, sine = phase_pair(
        two_pi / ctx_count * (counter[:, None] * target[None, :] % ctx_count).astype(jnp.float32)
    )
    matrix = jnp.stack([cosine, -sine])
    summed = jnp.einsum("opj,oxjs->xps", matrix, parts, precision=highest) / total_length
    local_conv = summed.astype(jnp.bfloat16)
    convolved = lax.all_to_all(local_conv, "ctx", split_axis=1, concat_axis=2, tiled=True).reshape(
        channel_count, seq_length
    )
    tokens_conv = lax.all_to_all(convolved, "chan", split_axis=1, concat_axis=0, tiled=True)
    result = gate_branch.astype(jnp.float32) * (
        tokens_conv.astype(jnp.float32) + skip_gain[:, None] * carried.astype(jnp.float32)
    )
    return result.astype(jnp.bfloat16)


lanes = 128
MESH = pl.DeviceIdType.MESH
VMEM = pl.BlockSpec(memory_space=pltpu.VMEM)


@functools.lru_cache(maxsize=None)
def transform_tables(rows_total, ctx_count, least_bytes):
    length = rows_total * lanes
    bit_count = ctx_count.bit_length() - 1
    rev = np.array([int(format(j, "b").zfill(bit_count)[::-1], 2) if bit_count else 0 for j in range(ctx_count)])
    a = np.arange(rows_total // ctx_count)
    k1 = (rev[:, None] + ctx_count * a[None, :]).reshape(-1)
    fold = lanes // (rows_total // ctx_count)
    k2 = np.arange(lanes).reshape(lanes // fold, fold).T.reshape(-1)
    n1, n2 = np.arange(rows_total), np.arange(lanes)
    f1 = np.exp(-2j * np.pi * (np.outer(k1, n1) % rows_total) / rows_total)
    f2 = np.exp(-2j * np.pi * (np.outer(n2, k2) % lanes) / lanes)
    tw = np.exp(-2j * np.pi * (np.outer(k1, n2) % length) / length)
    w1 = np.stack([f1.real, f1.imag])
    w2 = np.block([[f2.real, f2.imag], [-f2.imag, f2.real]])
    b2 = f2.conj().T
    w3 = np.block([[b2.real, b2.imag], [-b2.imag, b2.real]])
    b1 = f1.conj().T / length
    v1 = np.concatenate([b1.real, -b1.imag], axis=1)
    half = lambda t: np.asarray(t, dtype=jnp.bfloat16)
    pieces = [w1.reshape(2 * rows_total, rows_total), v1[:, :rows_total], v1[:, rows_total:]]
    square = np.concatenate([w2, w3], axis=1)
    pieces.append(np.pad(square, ((0, 0), (0, max(rows_total - square.shape[1], 0)))))
    turns = np.stack([tw.real, tw.imag]).astype(np.float32)
    spare = np.zeros((2 * (least_bytes // turns.nbytes),) + turns.shape[1:], np.float32)
    return np.concatenate(pieces).astype(jnp.bfloat16), np.concatenate([turns, spare])


def wrap(number, count):
    return number & (count - 1) if count & (count - 1) == 0 else lax.rem(number, count)


def over(number, count):
    return number >> (count.bit_length() - 1) if count & (count - 1) == 0 else number // count


def dot(a, b):
    return jnp.dot(a, b, preferred_element_type=jnp.float32)


def fused_kernel(ctx_count, chan_count, skip_hbm, v_hbm, k_hbm, gate_hbm, s_hbm, table_hbm, tw_hbm, out_ref, *refs):
    skip_ref, w1_ref, w2_ref, w3_ref, v1_ref, tw_ref = refs[:6]
    s_ref, stage, r_ref, x_ref, y_ref, g_ref, b_ref = refs[6:13]
    v_ref, k_ref, gate_ref, c_ref, o_ref = refs[13:18]
    sent, got_c, got_s, got_y, local, ready = refs[18:]
    ctx, chan = lax.axis_index("ctx"), lax.axis_index("chan")
    me = ctx * chan_count + chan
    total = ctx_count * chan_count
    pairs, rows = x_ref.shape[0], c_ref.shape[1]
    rows_total = x_ref.shape[1]
    block = stage.shape[2]
    local_channels = stage.shape[1]
    wide = 2 * lanes

    def load(index, source, target):
        return pltpu.make_async_copy(source, target, local.at[index])

    first_rows = 2 * rows_total
    share = 2 * ctx_count
    rest = local_channels - share
    loads = [
        load(0, v_hbm, v_ref),
        load(1, k_hbm, k_ref),
        load(2, s_hbm.at[pl.ds(0, share)], s_ref.at[pl.ds(0, share)]),
        load(3, table_hbm.at[pl.ds(0, first_rows)], w1_ref),
        load(4, table_hbm.at[pl.ds(2 * first_rows, wide), pl.ds(0, wide)], w2_ref),
        load(5, table_hbm.at[pl.ds(2 * first_rows, wide), pl.ds(wide, wide)], w3_ref),
        load(6, tw_hbm.at[pl.ds(0, 2)], tw_ref),
        load(7, table_hbm.at[pl.ds(first_rows, rows_total)], v1_ref.at[:, pl.ds(0, rows_total)]),
        load(8, table_hbm.at[pl.ds(first_rows + rows_total, rows_total)], v1_ref.at[:, pl.ds(rows_total, rows_total)]),
        load(9, gate_hbm, gate_ref),
        load(10, skip_hbm, skip_ref),
        load(11, s_hbm.at[pl.ds(local_channels, share)], s_ref.at[pl.ds(local_channels, share)]),
        load(12, s_hbm.at[pl.ds(share, rest)], s_ref.at[pl.ds(share, rest)]),
        load(13, s_hbm.at[pl.ds(local_channels + share, rest)], s_ref.at[pl.ds(local_channels + share, rest)]),
    ]
    barrier = pltpu.get_barrier_semaphore()
    even = lax.rem(ctx, 2) == 0
    partner = (ctx + 1 - 2 * lax.rem(ctx, 2), chan)

    def signal(semaphore, device):
        pl.semaphore_signal(semaphore, inc=1, device_id=device, device_id_type=MESH)

    for index in (0, 1, 2, 11):
        loads[index].start()

    @pl.loop(0, ctx_count // 2)
    def _(chip):
        @pl.when(2 * chip != ctx)
        def _():
            signal(barrier, (2 * chip, chan))

        @pl.loop(1, chan_count)
        def _(offset):
            signal(barrier, (2 * chip + 1, lax.rem(chan + offset, chan_count)))

    for index in (12, 13, 3, 4, 6, 5, 7, 8, 9, 10):
        loads[index].start()
    group = 2 * ctx_count

    def pack(pair):
        @pl.loop(0, chan_count)
        def _(chan_index):
            index = chan_index * pairs + pair
            at = pl.ds(pl.multiple_of(index * group, group), group)
            product = (k_ref[at].astype(jnp.float32) * v_ref[at].astype(jnp.float32)).astype(jnp.bfloat16)
            split = product.astype(jnp.float32).reshape(ctx_count, 2, rows, lanes)
            packed = jnp.concatenate([split[:, 0], split[:, 1]], axis=2)
            c_ref[pl.ds(index * ctx_count, ctx_count)] = packed.astype(jnp.bfloat16)

    def place(offset):
        other = wrap(me + offset, total)
        return other, over(other, chan_count), wrap(other, chan_count)

    def slot(ctx_index, chan_index, pair):
        return (chan_index * pairs + pair) * ctx_count + ctx_index

    my_rows = pl.ds(pl.multiple_of(me * rows, rows), rows)
    my_block = pl.ds(pl.multiple_of(ctx * block, block), block)

    def carried_copy(pair, offset):
        other, other_ctx, other_chan = place(offset)
        return pltpu.make_async_remote_copy(
            src_ref=c_ref.at[slot(other_ctx, other_chan, pair)],
            dst_ref=x_ref.at[pair, my_rows],
            send_sem=sent.at[0],
            recv_sem=got_c.at[pair],
            device_id=(other_ctx, other_chan),
            device_id_type=MESH,
        )

    def spectra_copy(pair, first, count, offset):
        other_ctx = wrap(ctx + offset, ctx_count)
        return pltpu.make_async_remote_copy(
            src_ref=stage.at[:, pl.ds((pair * ctx_count + other_ctx) * 2 + first, count)],
            dst_ref=r_ref.at[:, pl.ds(2 * pair + first, count), my_block],
            send_sem=sent.at[1],
            recv_sem=got_s.at[2 * pair + first],
            device_id=(other_ctx, chan),
            device_id_type=MESH,
        )

    def columns(first, count):
        return pl.ds(first * lanes, count * lanes)

    def result_copy(pair, first, count, other):
        other_ctx, other_chan = over(other, chan_count), wrap(other, chan_count)
        return pltpu.make_async_remote_copy(
            src_ref=y_ref.at[pair, pl.ds(pl.multiple_of(other * rows, rows), rows), columns(first, count)],
            dst_ref=o_ref.at[slot(ctx, chan, pair), :, columns(first, count)],
            send_sem=sent.at[2],
            recv_sem=got_y.at[pair, chan],
            device_id=(other_ctx, other_chan),
            device_id_type=MESH,
        )

    def settle(ref, sem):
        pltpu.make_async_copy(ref, ref, sem).wait()

    def turned(part, channel):
        flipped = s_ref[part * local_channels + channel].astype(jnp.bfloat16).T
        pieces = [flipped[f * block : (f + 1) * block] for f in range(flipped.shape[0] // block)]
        return jnp.concatenate(pieces, axis=1).astype(jnp.bfloat16)

    def turn(pair, begin, count):
        @pl.loop(1, ctx_count)
        def _(offset):
            first = (pair * ctx_count + lax.rem(ctx + offset, ctx_count)) * 2
            for part in range(2):
                for which in range(begin, begin + count):
                    stage[part, first + which] = turned(part, first + which)

    def turn_own(pair):
        for part in range(2):
            for which in range(2):
                r_ref[part, 2 * pair + which, my_block] = turned(part, (pair * ctx_count + ctx) * 2 + which)
        x_ref[pair, my_rows] = c_ref[slot(ctx, chan, pair)]

    def send_carried(pair):
        @pl.loop(1, total)
        def _(offset):
            carried_copy(pair, offset).start()

    def send_spectra(pair, first, count):
        @pl.loop(1, ctx_count)
        def _(offset):
            spectra_copy(pair, first, count, offset).start()

    chunk = 2 * lanes

    def forward(pair):
        settle(c_ref.at[pl.ds(0, total - 1)], got_c.at[pair])
        x = x_ref.at[pair]

        @pl.loop(0, rows_total // chunk)
        def _(step):
            at = pl.ds(pl.multiple_of(step * chunk, chunk), chunk)
            below = pl.ds(pl.multiple_of(rows_total + step * chunk, chunk), chunk)
            real, imag = dot(w1_ref[at], x[...]), dot(w1_ref[below], x[...])
            t_real, t_imag = tw_ref[0, at], tw_ref[1, at]
            for which in range(2):
                cols = slice(which * lanes, (which + 1) * lanes)
                a_real, a_imag = real[:, cols], imag[:, cols]
                twiddled = jnp.concatenate(
                    [a_real * t_real - a_imag * t_imag, a_real * t_imag + a_imag * t_real], axis=1
                )
                b_ref[2 * pair + which, at] = dot(twiddled.astype(jnp.bfloat16), w2_ref[...])

    def backward(pair, first, count):
        settle(stage.at[:, pl.ds(0, count * (ctx_count - 1))], got_s.at[2 * pair + first])

        @pl.loop(0, rows_total // chunk)
        def _(step):
            at = pl.ds(pl.multiple_of(step * chunk, chunk), chunk)
            below = pl.ds(pl.multiple_of(rows_total + step * chunk, chunk), chunk)
            t_real, t_imag = tw_ref[0, at], tw_ref[1, at]
            for which in range(first, first + count):
                cols = slice(which * lanes, (which + 1) * lanes)
                bins = b_ref[2 * pair + which, at]
                b_real, b_imag = bins[:, :lanes], bins[:, lanes:]
                f_real = r_ref[0, 2 * pair + which, at].astype(jnp.float32)
                f_imag = r_ref[1, 2 * pair + which, at].astype(jnp.float32)
                shaped = jnp.concatenate(
                    [b_real * f_real - b_imag * f_imag, b_real * f_imag + b_imag * f_real], axis=1
                )
                back = dot(shaped.astype(jnp.bfloat16), w3_ref[...])
                z_real, z_imag = back[:, :lanes], back[:, lanes:]
                g_ref[at, cols] = (z_real * t_real + z_imag * t_imag).astype(jnp.bfloat16)
                g_ref[below, cols] = (z_imag * t_real - z_real * t_imag).astype(jnp.bfloat16)

        steps = rows_total // lanes
        spread = total // steps
        home = me // spread
        cols = slice(first * lanes, (first + count) * lanes)

        @pl.loop(0, steps)
        def _(step):
            turn_of = lax.rem(home + 1 + step, steps)
            at = pl.ds(pl.multiple_of(turn_of * lanes, lanes), lanes)
            y_ref[pair, at, cols] = dot(v1_ref[at], g_ref[:, cols]).astype(jnp.bfloat16)

            @pl.loop(0, spread)
            def _(index):
                other = turn_of * spread + wrap(me + 1 + index, spread)

                @pl.when(other != me)
                def _():
                    result_copy(pair, first, count, other).start()

        o_ref[slot(ctx, chan, pair), :, cols] = y_ref[pair, my_rows, cols]

    def finish(pair):
        settle(o_ref.at[pl.ds(0, ctx_count - 1)], got_y.at[pair, chan])
        gate_group(pair, chan)

        @pl.loop(1, chan_count)
        def _(offset):
            chan_index = lax.rem(chan + offset, chan_count)
            settle(o_ref.at[pl.ds(0, ctx_count)], got_y.at[pair, chan_index])
            gate_group(pair, chan_index)

    def gate_group(pair, chan_index):
        first = slot(0, chan_index, pair)
        sums = []
        for i in range(ctx_count):
            for which in range(2):
                cols = slice(which * lanes, (which + 1) * lanes)
                carried = c_ref[first + i, :, cols].astype(jnp.float32)
                gain = skip_ref[2 * (first + i) + which]
                sums.append(o_ref[first + i, :, cols].astype(jnp.float32) + gain * carried)
        flat = jnp.stack(sums).reshape(group, rows * lanes)
        at = pl.ds(pl.multiple_of(first * 2, group), group)
        out_ref[at] = (gate_ref[at].astype(jnp.float32) * flat).astype(jnp.bfloat16)

    def meet_plane():
        @pl.when(even)
        def _():
            pl.semaphore_wait(barrier, ctx_count - 1)
            signal(ready, partner)

        @pl.when(jnp.logical_not(even))
        def _():
            pl.semaphore_wait(ready, 1)

    def meet_all():
        @pl.when(jnp.logical_not(even))
        def _():
            pl.semaphore_wait(barrier, ctx_count * (chan_count - 1))
            signal(ready, partner)

        @pl.when(even)
        def _():
            pl.semaphore_wait(ready, 1)

    waited = set()

    def need(*indices):
        for index in indices:
            if index not in waited:
                waited.add(index)
                loads[index].wait()

    need(0, 1)
    pack(0)
    need(0, 1)
    pack(1)
    need(0, 1)
    pack(2)
    meet_plane()
    meet_all()
    send_carried(0)
    send_carried(1)
    send_carried(2)
    need(2, 11)
    turn(0, 0, 1)
    send_spectra(0, 0, 1)
    need(2, 11)
    turn(0, 1, 1)
    send_spectra(0, 1, 1)
    need(12, 13)
    turn(1, 0, 1)
    send_spectra(1, 0, 1)
    need(12, 13)
    turn(1, 1, 1)
    send_spectra(1, 1, 1)
    need(12, 13)
    turn(2, 0, 2)
    send_spectra(2, 0, 1)
    send_spectra(2, 1, 1)
    need(2, 11)
    turn_own(0)
    need(3, 4, 6)
    forward(0)
    need(5, 7, 8)
    backward(0, 0, 1)
    need(12, 13)
    turn_own(1)
    need(3, 4, 6)
    forward(1)
    need(5, 7, 8)
    backward(0, 1, 1)
    need(5, 7, 8)
    backward(1, 0, 1)
    need(12, 13)
    turn_own(2)
    need(3, 4, 6)
    forward(2)
    need(5, 7, 8)
    backward(1, 1, 1)
    need(5, 7, 8)
    backward(2, 0, 1)
    need(5, 7, 8)
    backward(2, 1, 1)
    need(9, 10)
    finish(0)
    need(9, 10)
    finish(1)
    need(9, 10)
    finish(2)
    settle(c_ref.at[pl.ds(0, pairs * (total - 1))], sent.at[0])
    settle(stage.at[:, pl.ds(0, 2 * pairs * (ctx_count - 1))], sent.at[1])
    settle(o_ref.at[pl.ds(0, pairs * (total - 1))], sent.at[2])


def channel_body(value_branch, key_branch, gate_branch, skip_gain, spectra):
    channels, tokens = value_branch.shape
    ctx_count, chan_count = lax.axis_size("ctx"), lax.axis_size("chan")
    total = ctx_count * chan_count
    rows = tokens // lanes
    rows_total = rows * total
    pairs = channels // total // 2
    local_channels = spectra.shape[1]
    block = spectra.shape[3] // lanes
    table, turns = [jnp.asarray(t) for t in transform_tables(rows_total, ctx_count, 2 * channels * tokens)]
    sems = lambda *shape: pltpu.SemaphoreType.DMA(shape)
    hbm = pl.BlockSpec(memory_space=pl.ANY)
    packed = pltpu.VMEM((channels // 2, rows, 2 * lanes), jnp.bfloat16)
    held = pltpu.VMEM((channels, tokens), jnp.bfloat16)
    half = lambda *shape: pltpu.VMEM(shape, jnp.bfloat16)
    return pl.pallas_call(
        functools.partial(fused_kernel, ctx_count, chan_count),
        in_specs=[hbm] * 7,
        out_specs=VMEM,
        out_shape=jax.ShapeDtypeStruct((channels, tokens), jnp.bfloat16),
        scratch_shapes=[
            pltpu.SMEM((channels,), jnp.float32),
            half(2 * rows_total, rows_total),
            half(2 * lanes, 2 * lanes),
            half(2 * lanes, 2 * lanes),
            half(rows_total, 2 * rows_total),
            pltpu.VMEM((2, rows_total, lanes), jnp.float32),
            pltpu.VMEM((2 * local_channels, block, lanes), jnp.float32),
            half(2, local_channels, block, lanes),
            half(2, 2 * pairs, rows_total, lanes),
            half(pairs, rows_total, 2 * lanes),
            half(pairs, rows_total, 2 * lanes),
            half(2 * rows_total, 2 * lanes),
            pltpu.VMEM((2 * pairs, rows_total, 2 * lanes), jnp.float32),
            held, held, held, packed, packed,
            sems(3), sems(pairs), sems(2 * pairs), sems(pairs, chan_count), sems(14), pltpu.SemaphoreType.REGULAR,
        ],
        compiler_params=pltpu.CompilerParams(collective_id=0, has_side_effects=True, vmem_limit_bytes=55369728),
    )(
        pltpu.with_memory_space_constraint(skip_gain, pltpu.HBM),
        value_branch,
        key_branch,
        gate_branch,
        spectra.reshape(2 * local_channels, block, lanes),
        table,
        turns,
    )


def body(value_branch, key_branch, gate_branch, skip_gain, spectra):
    channels, tokens = value_branch.shape
    ctx_count, chan_count = lax.axis_size("ctx"), lax.axis_size("chan")
    total = ctx_count * chan_count
    block_rows = tokens * chan_count // lanes
    fits = (
        channels % (2 * total) == 0
        and ctx_count % 8 == 0
        and tokens % (16 * lanes) == 0
        and block_rows <= lanes
        and lanes % block_rows == 0
        and (tokens * total // lanes) % lanes == 0
    )
    chosen = channel_body if fits else blockwise_body
    return chosen(value_branch, key_branch, gate_branch, skip_gain, spectra)


def solution(mesh):
    in_specs = (
        P(None, ("ctx", "chan")),
        P(None, ("ctx", "chan")),
        P(None, ("ctx", "chan")),
        P(),
        P(None, "chan", "ctx", None),
    )
    out_specs = P(None, ("ctx", "chan"))
    return jax.shard_map(body, mesh=mesh, in_specs=in_specs, out_specs=out_specs, check_vma=False)
```

```python
import functools
import math

import jax
import jax.numpy as jnp
import numpy as np
from jax import lax
from jax.experimental import pallas as pl
from jax.experimental.pallas import tpu as pltpu
from jax.sharding import PartitionSpec as P

two_pi = 2.0 * math.pi
first_factor = 128
highest = lax.Precision.HIGHEST


def reversed_bits(numbers, bit_count):
    result = numbers * 0
    for bit_number in range(bit_count):
        result = result + (numbers >> bit_number & 1) * (1 << bit_count - 1 - bit_number)
    return result


def phase_pair(radians):
    return (jnp.cos(radians), jnp.sin(radians))


def block_table(length_of, direction):
    counter = jnp.arange(length_of, dtype=jnp.int32)
    product = counter[:, None] * counter[None, :] % length_of
    cosine, sine = phase_pair(direction * two_pi / length_of * product.astype(jnp.float32))
    upper_rows = jnp.stack([cosine, -sine], axis=1)
    lower_rows = jnp.stack([sine, cosine], axis=1)
    return jnp.stack([upper_rows, lower_rows], axis=0)


def complex_mul(signal, factor):
    factor_real, factor_imag = factor
    return jnp.stack(
        [
            signal[0] * factor_real - signal[1] * factor_imag,
            signal[0] * factor_imag + signal[1] * factor_real,
        ]
    )


def forward_local(signal):
    channel_count, seq_length = (signal.shape[1], signal.shape[2])
    second_factor = seq_length // first_factor
    blocked = signal.reshape(2, channel_count, first_factor, second_factor)
    section_one = jnp.einsum(
        "orca,cxaq->oxrq", block_table(first_factor, -1.0), blocked, precision=highest
    )
    column = jnp.arange(first_factor, dtype=jnp.int32)[:, None]
    within = jnp.arange(second_factor, dtype=jnp.int32)[None, :]
    twiddle = phase_pair(-two_pi / seq_length * (column * within).astype(jnp.float32))
    section_two = complex_mul(section_one, twiddle)
    section_three = jnp.einsum(
        "peoq,oxrq->pxer", block_table(second_factor, -1.0), section_two, precision=highest
    )
    return section_three.reshape(2, channel_count, seq_length)


def inverse_local(signal):
    channel_count, seq_length = (signal.shape[1], signal.shape[2])
    second_factor = seq_length // first_factor
    blocked = signal.reshape(2, channel_count, second_factor, first_factor)
    section_one = jnp.einsum(
        "pqoe,oxer->pxqr", block_table(second_factor, 1.0), blocked, precision=highest
    )
    within = jnp.arange(second_factor, dtype=jnp.int32)[:, None]
    column = jnp.arange(first_factor, dtype=jnp.int32)[None, :]
    twiddle = phase_pair(two_pi / seq_length * (within * column).astype(jnp.float32))
    section_two = complex_mul(section_one, twiddle)
    section_three = jnp.einsum(
        "paor,oxqr->pxaq", block_table(first_factor, 1.0), section_two, precision=highest
    )
    return section_three.reshape(2, channel_count, seq_length)


def blockwise_body(value_branch, key_branch, gate_branch, skip_gain, spectra):
    carried = (key_branch.astype(jnp.float32) * value_branch.astype(jnp.float32)).astype(
        jnp.bfloat16
    )
    series = lax.all_to_all(carried, "chan", split_axis=0, concat_axis=1, tiled=True)
    channel_count, seq_length = series.shape
    ctx_count = lax.axis_size("ctx")
    bit_count = ctx_count.bit_length() - 1
    device = lax.axis_index("ctx")
    total_length = seq_length * ctx_count
    counter = jnp.arange(ctx_count, dtype=jnp.int32)
    target = reversed_bits(counter, bit_count)
    blocks = lax.all_to_all(
        series.reshape(channel_count, 1, seq_length), "ctx", split_axis=2, concat_axis=1, tiled=True
    )
    matrix = jnp.stack(
        phase_pair(
            -two_pi
            / ctx_count
            * (target[:, None] * counter[None, :] % ctx_count).astype(jnp.float32)
        )
    )
    rows = jnp.einsum("ojp,xps->oxjs", matrix, blocks.astype(jnp.float32), precision=highest)
    received = lax.all_to_all(rows, "ctx", split_axis=2, concat_axis=3, tiled=True)
    signal = received.reshape(2, channel_count, seq_length)
    device_rank = reversed_bits(device, bit_count)
    positions = jnp.arange(seq_length, dtype=jnp.int32)
    radians = two_pi / total_length * (positions * device_rank).astype(jnp.float32)
    signal = complex_mul(signal, phase_pair(-radians))
    spectrum = forward_local(signal)
    shaped = complex_mul(spectrum, (spectra[0, :, 0, :], spectra[1, :, 0, :]))
    returned = complex_mul(inverse_local(shaped), phase_pair(radians))
    parts = lax.all_to_all(
        returned.reshape(2, channel_count, 1, seq_length),
        "ctx",
        split_axis=3,
        concat_axis=2,
        tiled=True,
    )
    cosine, sine = phase_pair(
        two_pi / ctx_count * (counter[:, None] * target[None, :] % ctx_count).astype(jnp.float32)
    )
    matrix = jnp.stack([cosine, -sine])
    summed = jnp.einsum("opj,oxjs->xps", matrix, parts, precision=highest) / total_length
    local_conv = summed.astype(jnp.bfloat16)
    convolved = lax.all_to_all(local_conv, "ctx", split_axis=1, concat_axis=2, tiled=True).reshape(
        channel_count, seq_length
    )
    tokens_conv = lax.all_to_all(convolved, "chan", split_axis=1, concat_axis=0, tiled=True)
    result = gate_branch.astype(jnp.float32) * (
        tokens_conv.astype(jnp.float32) + skip_gain[:, None] * carried.astype(jnp.float32)
    )
    return result.astype(jnp.bfloat16)


lanes = 128
MESH = pl.DeviceIdType.MESH
VMEM = pl.BlockSpec(memory_space=pltpu.VMEM)


@functools.lru_cache(maxsize=None)
def transform_tables(rows_total, ctx_count, least_bytes):
    length = rows_total * lanes
    bit_count = ctx_count.bit_length() - 1
    rev = np.array([int(format(j, "b").zfill(bit_count)[::-1], 2) if bit_count else 0 for j in range(ctx_count)])
    a = np.arange(rows_total // ctx_count)
    k1 = (rev[:, None] + ctx_count * a[None, :]).reshape(-1)
    fold = lanes // (rows_total // ctx_count)
    k2 = np.arange(lanes).reshape(lanes // fold, fold).T.reshape(-1)
    n1, n2 = np.arange(rows_total), np.arange(lanes)
    f1 = np.exp(-2j * np.pi * (np.outer(k1, n1) % rows_total) / rows_total)
    f2 = np.exp(-2j * np.pi * (np.outer(n2, k2) % lanes) / lanes)
    tw = np.exp(-2j * np.pi * (np.outer(k1, n2) % length) / length)
    w1 = np.stack([f1.real, f1.imag])
    w2 = np.block([[f2.real, f2.imag], [-f2.imag, f2.real]])
    b2 = f2.conj().T
    w3 = np.block([[b2.real, b2.imag], [-b2.imag, b2.real]])
    b1 = f1.conj().T / length
    v1 = np.concatenate([b1.real, -b1.imag], axis=1)
    half = lambda t: np.asarray(t, dtype=jnp.bfloat16)
    pieces = [w1.reshape(2 * rows_total, rows_total), v1[:, :rows_total], v1[:, rows_total:]]
    square = np.concatenate([w2, w3], axis=1)
    pieces.append(np.pad(square, ((0, 0), (0, max(rows_total - square.shape[1], 0)))))
    turns = np.stack([tw.real, tw.imag]).astype(np.float32)
    spare = np.zeros((2 * (least_bytes // turns.nbytes),) + turns.shape[1:], np.float32)
    return np.concatenate(pieces).astype(jnp.bfloat16), np.concatenate([turns, spare])


def wrap(number, count):
    return number & (count - 1) if count & (count - 1) == 0 else lax.rem(number, count)


def over(number, count):
    return number >> (count.bit_length() - 1) if count & (count - 1) == 0 else number // count


def dot(a, b):
    return jnp.dot(a, b, preferred_element_type=jnp.float32)


def fused_kernel(ctx_count, chan_count, skip_hbm, v_hbm, k_hbm, gate_hbm, s_hbm, table_hbm, tw_hbm, out_ref, *refs):
    skip_ref, w1_ref, w2_ref, w3_ref, v1_ref, tw_ref = refs[:6]
    s_ref, stage, r_ref, x_ref, y_ref, g_ref, b_ref = refs[6:13]
    v_ref, k_ref, gate_ref, c_ref, o_ref = refs[13:18]
    sent, got_c, got_s, got_y, local, ready = refs[18:]
    ctx, chan = lax.axis_index("ctx"), lax.axis_index("chan")
    me = ctx * chan_count + chan
    total = ctx_count * chan_count
    pairs, rows = x_ref.shape[0], c_ref.shape[1]
    rows_total = x_ref.shape[1]
    block = stage.shape[2]
    local_channels = stage.shape[1]
    wide = 2 * lanes

    def load(index, source, target):
        return pltpu.make_async_copy(source, target, local.at[index])

    first_rows = 2 * rows_total
    share = 2 * ctx_count
    rest = local_channels - share
    loads = [
        load(0, v_hbm, v_ref),
        load(1, k_hbm, k_ref),
        load(2, s_hbm.at[pl.ds(0, share)], s_ref.at[pl.ds(0, share)]),
        load(3, table_hbm.at[pl.ds(0, first_rows)], w1_ref),
        load(4, table_hbm.at[pl.ds(2 * first_rows, wide), pl.ds(0, wide)], w2_ref),
        load(5, table_hbm.at[pl.ds(2 * first_rows, wide), pl.ds(wide, wide)], w3_ref),
        load(6, tw_hbm.at[pl.ds(0, 2)], tw_ref),
        load(7, table_hbm.at[pl.ds(first_rows, rows_total)], v1_ref.at[:, pl.ds(0, rows_total)]),
        load(8, table_hbm.at[pl.ds(first_rows + rows_total, rows_total)], v1_ref.at[:, pl.ds(rows_total, rows_total)]),
        load(9, gate_hbm, gate_ref),
        load(10, skip_hbm, skip_ref),
        load(11, s_hbm.at[pl.ds(local_channels, share)], s_ref.at[pl.ds(local_channels, share)]),
        load(12, s_hbm.at[pl.ds(share, rest)], s_ref.at[pl.ds(share, rest)]),
        load(13, s_hbm.at[pl.ds(local_channels + share, rest)], s_ref.at[pl.ds(local_channels + share, rest)]),
    ]
    barrier = pltpu.get_barrier_semaphore()
    even = lax.rem(ctx, 2) == 0
    partner = (ctx + 1 - 2 * lax.rem(ctx, 2), chan)

    def signal(semaphore, device):
        pl.semaphore_signal(semaphore, inc=1, device_id=device, device_id_type=MESH)

    for index in (0, 1, 2, 11):
        loads[index].start()

    @pl.loop(0, ctx_count // 2)
    def _(chip):
        @pl.when(2 * chip != ctx)
        def _():
            signal(barrier, (2 * chip, chan))

        @pl.loop(1, chan_count)
        def _(offset):
            signal(barrier, (2 * chip + 1, lax.rem(chan + offset, chan_count)))

    for index in (12, 13, 3, 4, 6, 5, 7, 8, 9, 10):
        loads[index].start()
    group = 2 * ctx_count

    def pack(pair):
        @pl.loop(0, chan_count)
        def _(chan_index):
            index = chan_index * pairs + pair
            at = pl.ds(pl.multiple_of(index * group, group), group)
            product = (k_ref[at].astype(jnp.float32) * v_ref[at].astype(jnp.float32)).astype(jnp.bfloat16)
            split = product.astype(jnp.float32).reshape(ctx_count, 2, rows, lanes)
            packed = jnp.concatenate([split[:, 0], split[:, 1]], axis=2)
            c_ref[pl.ds(index * ctx_count, ctx_count)] = packed.astype(jnp.bfloat16)

    def place(offset):
        other = wrap(me + offset, total)
        return other, over(other, chan_count), wrap(other, chan_count)

    def slot(ctx_index, chan_index, pair):
        return (chan_index * pairs + pair) * ctx_count + ctx_index

    my_rows = pl.ds(pl.multiple_of(me * rows, rows), rows)
    my_block = pl.ds(pl.multiple_of(ctx * block, block), block)

    def carried_copy(pair, offset):
        other, other_ctx, other_chan = place(offset)
        return pltpu.make_async_remote_copy(
            src_ref=c_ref.at[slot(other_ctx, other_chan, pair)],
            dst_ref=x_ref.at[pair, my_rows],
            send_sem=sent.at[0],
            recv_sem=got_c.at[pair],
            device_id=(other_ctx, other_chan),
            device_id_type=MESH,
        )

    def spectra_copy(pair, first, count, offset):
        other_ctx = wrap(ctx + offset, ctx_count)
        return pltpu.make_async_remote_copy(
            src_ref=stage.at[:, pl.ds((pair * ctx_count + other_ctx) * 2 + first, count)],
            dst_ref=r_ref.at[:, pl.ds(2 * pair + first, count), my_block],
            send_sem=sent.at[1],
            recv_sem=got_s.at[2 * pair + first],
            device_id=(other_ctx, chan),
            device_id_type=MESH,
        )

    def columns(first, count):
        return pl.ds(first * lanes, count * lanes)

    def result_copy(pair, first, count, other):
        other_ctx, other_chan = over(other, chan_count), wrap(other, chan_count)
        return pltpu.make_async_remote_copy(
            src_ref=y_ref.at[pair, pl.ds(pl.multiple_of(other * rows, rows), rows), columns(first, count)],
            dst_ref=o_ref.at[slot(ctx, chan, pair), :, columns(first, count)],
            send_sem=sent.at[2],
            recv_sem=got_y.at[pair, chan],
            device_id=(other_ctx, other_chan),
            device_id_type=MESH,
        )

    def settle(ref, sem):
        pltpu.make_async_copy(ref, ref, sem).wait()

    def turned(part, channel):
        flipped = s_ref[part * local_channels + channel].astype(jnp.bfloat16).T
        pieces = [flipped[f * block : (f + 1) * block] for f in range(flipped.shape[0] // block)]
        return jnp.concatenate(pieces, axis=1).astype(jnp.bfloat16)

    def turn(pair, begin, count):
        @pl.loop(1, ctx_count)
        def _(offset):
            first = (pair * ctx_count + lax.rem(ctx + offset, ctx_count)) * 2
            for part in range(2):
                for which in range(begin, begin + count):
                    stage[part, first + which] = turned(part, first + which)

    def turn_own(pair):
        for part in range(2):
            for which in range(2):
                r_ref[part, 2 * pair + which, my_block] = turned(part, (pair * ctx_count + ctx) * 2 + which)
        x_ref[pair, my_rows] = c_ref[slot(ctx, chan, pair)]

    def send_carried(pair):
        @pl.loop(1, total)
        def _(offset):
            carried_copy(pair, offset).start()

    def send_spectra(pair, first, count):
        @pl.loop(1, ctx_count)
        def _(offset):
            spectra_copy(pair, first, count, offset).start()

    chunk = 2 * lanes

    def forward(pair):
        settle(c_ref.at[pl.ds(0, total - 1)], got_c.at[pair])
        x = x_ref.at[pair]

        @pl.loop(0, rows_total // chunk)
        def _(step):
            at = pl.ds(pl.multiple_of(step * chunk, chunk), chunk)
            below = pl.ds(pl.multiple_of(rows_total + step * chunk, chunk), chunk)
            real, imag = dot(w1_ref[at], x[...]), dot(w1_ref[below], x[...])
            t_real, t_imag = tw_ref[0, at], tw_ref[1, at]
            for which in range(2):
                cols = slice(which * lanes, (which + 1) * lanes)
                a_real, a_imag = real[:, cols], imag[:, cols]
                twiddled = jnp.concatenate(
                    [a_real * t_real - a_imag * t_imag, a_real * t_imag + a_imag * t_real], axis=1
                )
                b_ref[2 * pair + which, at] = dot(twiddled.astype(jnp.bfloat16), w2_ref[...])

    def backward(pair, first, count):
        settle(stage.at[:, pl.ds(0, count * (ctx_count - 1))], got_s.at[2 * pair + first])

        @pl.loop(0, rows_total // chunk)
        def _(step):
            at = pl.ds(pl.multiple_of(step * chunk, chunk), chunk)
            below = pl.ds(pl.multiple_of(rows_total + step * chunk, chunk), chunk)
            t_real, t_imag = tw_ref[0, at], tw_ref[1, at]
            for which in range(first, first + count):
                cols = slice(which * lanes, (which + 1) * lanes)
                bins = b_ref[2 * pair + which, at]
                b_real, b_imag = bins[:, :lanes], bins[:, lanes:]
                f_real = r_ref[0, 2 * pair + which, at].astype(jnp.float32)
                f_imag = r_ref[1, 2 * pair + which, at].astype(jnp.float32)
                shaped = jnp.concatenate(
                    [b_real * f_real - b_imag * f_imag, b_real * f_imag + b_imag * f_real], axis=1
                )
                back = dot(shaped.astype(jnp.bfloat16), w3_ref[...])
                z_real, z_imag = back[:, :lanes], back[:, lanes:]
                g_ref[at, cols] = (z_real * t_real + z_imag * t_imag).astype(jnp.bfloat16)
                g_ref[below, cols] = (z_imag * t_real - z_real * t_imag).astype(jnp.bfloat16)

        steps = rows_total // lanes
        spread = total // steps
        home = me // spread
        cols = slice(first * lanes, (first + count) * lanes)

        @pl.loop(0, steps)
        def _(step):
            turn_of = lax.rem(home + 1 + step, steps)
            at = pl.ds(pl.multiple_of(turn_of * lanes, lanes), lanes)
            y_ref[pair, at, cols] = dot(v1_ref[at], g_ref[:, cols]).astype(jnp.bfloat16)

            @pl.loop(0, spread)
            def _(index):
                other = turn_of * spread + wrap(me + 1 + index, spread)

                @pl.when(other != me)
                def _():
                    result_copy(pair, first, count, other).start()

        o_ref[slot(ctx, chan, pair), :, cols] = y_ref[pair, my_rows, cols]

    def finish(pair):
        settle(o_ref.at[pl.ds(0, ctx_count - 1)], got_y.at[pair, chan])
        gate_group(pair, chan)

        @pl.loop(1, chan_count)
        def _(offset):
            chan_index = lax.rem(chan + offset, chan_count)
            settle(o_ref.at[pl.ds(0, ctx_count)], got_y.at[pair, chan_index])
            gate_group(pair, chan_index)

    def gate_group(pair, chan_index):
        first = slot(0, chan_index, pair)
        sums = []
        for i in range(ctx_count):
            for which in range(2):
                cols = slice(which * lanes, (which + 1) * lanes)
                carried = c_ref[first + i, :, cols].astype(jnp.float32)
                gain = skip_ref[2 * (first + i) + which]
                sums.append(o_ref[first + i, :, cols].astype(jnp.float32) + gain * carried)
        flat = jnp.stack(sums).reshape(group, rows * lanes)
        at = pl.ds(pl.multiple_of(first * 2, group), group)
        out_ref[at] = (gate_ref[at].astype(jnp.float32) * flat).astype(jnp.bfloat16)

    def meet_plane():
        @pl.when(even)
        def _():
            pl.semaphore_wait(barrier, ctx_count - 1)
            signal(ready, partner)

        @pl.when(jnp.logical_not(even))
        def _():
            pl.semaphore_wait(ready, 1)

    def meet_all():
        @pl.when(jnp.logical_not(even))
        def _():
            pl.semaphore_wait(barrier, ctx_count * (chan_count - 1))
            signal(ready, partner)

        @pl.when(even)
        def _():
            pl.semaphore_wait(ready, 1)

    waited = set()

    def need(*indices):
        for index in indices:
            if index not in waited:
                waited.add(index)
                loads[index].wait()

    need(0, 1)
    pack(0)
    meet_plane()
    meet_all()
    send_carried(0)
    need(0, 1)
    pack(1)
    send_carried(1)
    need(0, 1)
    pack(2)
    send_carried(2)
    need(2, 11)
    turn(0, 0, 1)
    send_spectra(0, 0, 1)
    need(2, 11)
    turn(0, 1, 1)
    send_spectra(0, 1, 1)
    need(12, 13)
    turn(1, 0, 1)
    send_spectra(1, 0, 1)
    need(12, 13)
    turn(1, 1, 1)
    send_spectra(1, 1, 1)
    need(12, 13)
    turn(2, 0, 2)
    send_spectra(2, 0, 1)
    send_spectra(2, 1, 1)
    need(2, 11)
    turn_own(0)
    need(3, 4, 6)
    forward(0)
    need(5, 7, 8)
    backward(0, 0, 1)
    need(12, 13)
    turn_own(1)
    need(3, 4, 6)
    forward(1)
    need(5, 7, 8)
    backward(0, 1, 1)
    need(5, 7, 8)
    backward(1, 0, 1)
    need(12, 13)
    turn_own(2)
    need(3, 4, 6)
    forward(2)
    need(5, 7, 8)
    backward(1, 1, 1)
    need(5, 7, 8)
    backward(2, 0, 1)
    need(5, 7, 8)
    backward(2, 1, 1)
    need(9, 10)
    finish(0)
    need(9, 10)
    finish(1)
    need(9, 10)
    finish(2)
    settle(c_ref.at[pl.ds(0, pairs * (total - 1))], sent.at[0])
    settle(stage.at[:, pl.ds(0, 2 * pairs * (ctx_count - 1))], sent.at[1])
    settle(o_ref.at[pl.ds(0, pairs * (total - 1))], sent.at[2])


def channel_body(value_branch, key_branch, gate_branch, skip_gain, spectra):
    channels, tokens = value_branch.shape
    ctx_count, chan_count = lax.axis_size("ctx"), lax.axis_size("chan")
    total = ctx_count * chan_count
    rows = tokens // lanes
    rows_total = rows * total
    pairs = channels // total // 2
    local_channels = spectra.shape[1]
    block = spectra.shape[3] // lanes
    table, turns = [jnp.asarray(t) for t in transform_tables(rows_total, ctx_count, 2 * channels * tokens)]
    sems = lambda *shape: pltpu.SemaphoreType.DMA(shape)
    hbm = pl.BlockSpec(memory_space=pl.ANY)
    packed = pltpu.VMEM((channels // 2, rows, 2 * lanes), jnp.bfloat16)
    held = pltpu.VMEM((channels, tokens), jnp.bfloat16)
    half = lambda *shape: pltpu.VMEM(shape, jnp.bfloat16)
    return pl.pallas_call(
        functools.partial(fused_kernel, ctx_count, chan_count),
        in_specs=[hbm] * 7,
        out_specs=VMEM,
        out_shape=jax.ShapeDtypeStruct((channels, tokens), jnp.bfloat16),
        scratch_shapes=[
            pltpu.SMEM((channels,), jnp.float32),
            half(2 * rows_total, rows_total),
            half(2 * lanes, 2 * lanes),
            half(2 * lanes, 2 * lanes),
            half(rows_total, 2 * rows_total),
            pltpu.VMEM((2, rows_total, lanes), jnp.float32),
            pltpu.VMEM((2 * local_channels, block, lanes), jnp.float32),
            half(2, local_channels, block, lanes),
            half(2, 2 * pairs, rows_total, lanes),
            half(pairs, rows_total, 2 * lanes),
            half(pairs, rows_total, 2 * lanes),
            half(2 * rows_total, 2 * lanes),
            pltpu.VMEM((2 * pairs, rows_total, 2 * lanes), jnp.float32),
            held, held, held, packed, packed,
            sems(3), sems(pairs), sems(2 * pairs), sems(pairs, chan_count), sems(14), pltpu.SemaphoreType.REGULAR,
        ],
        compiler_params=pltpu.CompilerParams(collective_id=0, has_side_effects=True, vmem_limit_bytes=55369728),
    )(
        pltpu.with_memory_space_constraint(skip_gain, pltpu.HBM),
        value_branch,
        key_branch,
        gate_branch,
        spectra.reshape(2 * local_channels, block, lanes),
        table,
        turns,
    )


def body(value_branch, key_branch, gate_branch, skip_gain, spectra):
    channels, tokens = value_branch.shape
    ctx_count, chan_count = lax.axis_size("ctx"), lax.axis_size("chan")
    total = ctx_count * chan_count
    block_rows = tokens * chan_count // lanes
    fits = (
        channels % (2 * total) == 0
        and ctx_count % 8 == 0
        and tokens % (16 * lanes) == 0
        and block_rows <= lanes
        and lanes % block_rows == 0
        and (tokens * total // lanes) % lanes == 0
    )
    chosen = channel_body if fits else blockwise_body
    return chosen(value_branch, key_branch, gate_branch, skip_gain, spectra)


def solution(mesh):
    in_specs = (
        P(None, ("ctx", "chan")),
        P(None, ("ctx", "chan")),
        P(None, ("ctx", "chan")),
        P(),
        P(None, "chan", "ctx", None),
    )
    out_specs = P(None, ("ctx", "chan"))
    return jax.shard_map(body, mesh=mesh, in_specs=in_specs, out_specs=out_specs, check_vma=False)
```
